512 devices in a mesh: row: 16 (over x, y), col: 32 (over z, core).
Axes of the slice: x: 4, y: 4, z: 16, core: 2. Of those that a mesh axis runs over, the one named last changes fastest.
Arguments:
- trail_adjoint: float32 [8, 2048, 4, 4096], P(None, 'row', None, 'col'), may hold values from -6 to 6
- panel: float32 [8, 2048, 128], P(None, 'row'), may hold values from -0.046875 to 0.046875
- panel_adjoint: float32 [8, 2048, 128], P(None, 'row'), may hold values from -6 to 6
- diag_block: float32 [128, 128], replicated, as said below
Outputs:
- input_adjoint: float32 [8, 2048, 128], P(None, 'row')
- block_adjoint: float32 [128, 128], replicated
The draws below stay inside these ranges and needn't reach their ends.
Inputs may be any that keep to these rules, and one draw needn't show every extreme that they name: diag_block is lower triangular with diagonal entries between 1.5 and 3 and zeros above the diagonal.
All inputs are finite; a program needn't handle non-finite values.
Results may differ from the reference program's by a relative error of at most 0.000082.
Values sent between devices are 32-bit elements; how exact they have to be, the bound alone decides.
A program may use at most 64 MiB of HBM per device.

```python
import jax
import jax.numpy as jnp
from jax import lax

M = 16384
BLK = 128
RB = 8
CB = 4
N_ROW = 16
N_COL = 32


def draw_diag_block(key, part):
    first, second = jax.random.split(jax.random.fold_in(key, 11))
    lower_part = jax.random.normal(first, (BLK, BLK), jnp.float32) * (1.0 / BLK) ** 0.5
    diagonal = jax.random.uniform(second, (BLK,), jnp.float32, 1.5, 3.0)
    return jnp.tril(lower_part, -1) + jnp.diag(diagonal)


def block_levels(key, shape, cuts, low, top_value):
    loudness, own = 1.0, jax.random.fold_in(key, 6)
    for axis_at, shards_of in cuts:
        draws = jnp.exp(jax.random.uniform(jax.random.fold_in(own, axis_at), (shards_of,), jnp.float32, low / len(cuts), top_value / len(cuts)))
        loudness = loudness * jnp.repeat(draws, shape[axis_at] // shards_of).reshape([-1 if axis == axis_at else 1 for axis in range(len(shape))])
    return loudness


def centred(own_key, dims, width, bound, shards=(), held_as=jnp.bfloat16):
    drawn = jax.random.normal(own_key, dims, jnp.float32) * width
    if len(shards) > 0:
        drawn = block_levels(own_key, dims, shards, -0.22, 0.18) * drawn
    return jnp.clip(drawn, min=-bound, max=bound).astype(held_as)


def setup_inputs(seed: int = 0) -> dict:
    keys = jax.random.split(jax.random.key(seed), 5)
    trail_adjoint = centred(keys[0], (RB, N_ROW * BLK, CB, N_COL * BLK), 1.0, 6.0, ((1, 16), (3, 32)), jnp.float32)
    panel = centred(keys[1], (RB, N_ROW * BLK, BLK), M ** -0.5, 0.046875, ((1, 16),), jnp.float32)
    panel_adjoint = centred(keys[2], (RB, N_ROW * BLK, BLK), 1.0, 6.0, ((1, 16),), jnp.float32)
    diag_block = draw_diag_block(jax.random.fold_in(keys[4], 71), 0)
    return {"trail_adjoint": trail_adjoint, "panel": panel, "panel_adjoint": panel_adjoint, "diag_block": diag_block}


def reference(trail_adjoint, panel, panel_adjoint, diag_block):
    whole = trail_adjoint.reshape(M, M)
    factor = panel.reshape(M, BLK)
    given = panel_adjoint.reshape(M, BLK)
    direct = jnp.dot(whole.astype(jnp.float32), factor.astype(jnp.float32), precision=lax.Precision.HIGHEST, preferred_element_type=jnp.float32)
    flipped = jnp.dot(whole.T.astype(jnp.float32), factor.astype(jnp.float32), precision=lax.Precision.HIGHEST, preferred_element_type=jnp.float32)
    total = given - (direct + flipped)
    solved = lax.linalg.triangular_solve(diag_block, total, left_side=False, lower=True)
    gram = -jnp.dot(solved.T.astype(jnp.float32), factor.astype(jnp.float32), precision=lax.Precision.HIGHEST, preferred_element_type=jnp.float32)
    return (solved.reshape(RB, N_ROW * BLK, BLK), jnp.tril(gram))
```

```python
import functools

import jax
import jax.numpy as jnp
from jax import lax
from jax.experimental import pallas as pl
from jax.experimental.pallas import tpu as pltpu
from jax.sharding import PartitionSpec as P

MESH = pl.DeviceIdType.MESH
F32 = jnp.float32
HI = lax.Precision.HIGHEST
BLK = 128


def dot(a, b):
    return jnp.dot(a, b, precision=HI, preferred_element_type=F32)


def dot_t(a, b):
    return lax.dot_general(
        a, b, (((0,), (0,)), ((), ())), precision=HI, preferred_element_type=F32
    )


def invert_lower(d):
    n = d.shape[0]
    row = lax.broadcasted_iota(jnp.int32, (n, n), 0)
    col = lax.broadcasted_iota(jnp.int32, (n, n), 1)
    eye = row == col
    zero = jnp.zeros_like(d)
    diag = jnp.where(eye, d, zero)
    recip_row = 1.0 / jnp.sum(diag, axis=1, keepdims=True)
    recip_col = 1.0 / jnp.sum(diag, axis=0, keepdims=True)

    def below(shift):
        same = lax.shift_right_logical(row, shift + 1) == lax.shift_right_logical(col, shift + 1)
        other = lax.shift_right_logical(row, shift) != lax.shift_right_logical(col, shift)
        return jnp.where(same & other & (row > col), d, zero)

    inv = jnp.where(eye, jnp.broadcast_to(recip_row, (n, n)), -(below(0) * recip_row) * recip_col)
    shift = 1
    while (1 << shift) < n:
        inv = inv - dot(inv, dot(below(shift), inv))
        shift += 1
    return inv


def kernel(
    rows,
    cols,
    s_hbm,
    panel_hbm,
    given_hbm,
    diag_hbm,
    x_out,
    g_out,
    s_v,
    p_v,
    b_v,
    d_v,
    pt_v,
    inv_v,
    lc,
    flip_v,
    flip_in,
    route_src,
    route_in,
    half_v,
    give_v,
    pair_in,
    agg_far,
    agg_near,
    agg_out,
    fin_in,
    x_v,
    prod_v,
    prod_in,
    psum_v,
    psum_in,
    ppair_v,
    ppair_in,
    pfull_v,
    gram_v,
    loc,
    sc_s,
    sc_r,
    ag_s,
    ag_r,
    fl_s,
    fl_r,
    rt_s,
    rt_r,
    pr_s,
    pr_r,
    rs_s,
    rs_r,
    x_s,
    x_r,
    xp_s,
    xp_r,
    g_s,
    g_r,
):
    R, C = rows, cols
    Z = C // 2
    W = Z // 4
    SL = 8 * BLK // C
    NS = BLK // SL
    HALF = 4 * NS
    r = lax.axis_index("row")
    c = lax.axis_index("col")
    z = c // 2
    k = c % 2

    def dev(row, chip, core):
        return (row, chip * 2 + core)

    def copy(src, dst, send, recv, device):
        return pltpu.make_async_remote_copy(
            src_ref=src,
            dst_ref=dst,
            send_sem=send,
            recv_sem=recv,
            device_id=device,
            device_id_type=MESH,
        )

    def wait(ref, sem):
        pltpu.make_async_copy(ref, ref, sem).wait()

    def offset_of(row, chip):
        return (chip - row // 2 + R // 4 + Z) % Z

    def slice_in_half(o):
        m = o % (R // 2)
        return (2 * (m // NS) + o // (R // 2)) * NS + m % NS

    cp_panel = pltpu.make_async_copy(panel_hbm, p_v, loc.at[0])
    cp_panel.start()
    cp_s = []
    for a in range(8):
        cp_s.append(pltpu.make_async_copy(s_hbm.at[a], s_v.at[a], loc.at[1 + a]))
        cp_s[a].start()
    my_slice = slice_in_half(offset_of(r, z))
    sid = k * HALF + my_slice
    cp_b = pltpu.make_async_copy(given_hbm.at[sid], b_v, loc.at[9])
    cp_b.start()
    cp_d = pltpu.make_async_copy(diag_hbm, d_v, loc.at[10])
    cp_d.start()

    to_r = c % R
    to_z = (z - R // 4 + r % (R // 2) + Z) % Z
    to_k = r // (R // 2)
    to_self = (to_r == r) & (to_z == z) & (to_k == k)
    off = offset_of(r, z)
    from_r = k * (R // 2) + off % (R // 2)
    from_c = r + R * (off // (R // 2))

    barrier = pltpu.get_barrier_semaphore()
    for i in range(1, R):
        pl.semaphore_signal(barrier, inc=1, device_id=((r + i) % R, c), device_id_type=MESH)
    for i in range(1, Z):
        pl.semaphore_signal(barrier, inc=1, device_id=dev(r, (z + i) % Z, k), device_id_type=MESH)
    pl.semaphore_signal(barrier, inc=1, device_id=dev(r, z, 1 - k), device_id_type=MESH)
    pl.semaphore_signal(barrier, inc=1, device_id=(from_r, from_c), device_id_type=MESH)
    pl.semaphore_wait(barrier, R - 1 + Z - 1 + 2)

    owner = c % R
    which = c // R
    own = owner == r

    def piece(s):
        return panel_hbm.at[(2 * (s // NS) + which) * NS + s % NS]

    @pl.when(own)
    def _():
        for i in range(1, R):
            s = (r + i) % R
            copy(piece(s), lc.at[s], sc_s, sc_r, (s, c)).start()
        mine = pltpu.make_async_copy(piece(r), lc.at[r], loc.at[11])
        mine.start()
        mine.wait()

    cp_panel.wait()
    for a in range(8):
        block = p_v[pl.ds(a * NS, NS)].reshape(BLK, BLK)
        pt_v[:, pl.ds(a * BLK, BLK)] = block.T
    for a in range(8):
        cp_s[a].wait()
    for b in range(4):
        tall = jnp.concatenate([s_v[a, pl.ds(b, BLK, stride=4), :] for a in range(8)], axis=0)
        part = dot(pt_v[...], tall)
        flip_v[pl.ds(b * NS, NS)] = part.T.reshape(NS, SL, BLK)
    for i in range(1, R):
        s = (r + i) % R
        copy(flip_v.at[s], flip_in.at[r], fl_s, fl_r, (s, c)).start()

    @pl.when(jnp.logical_not(own))
    def _():
        wait(lc.at[r], sc_r)

    for i in range(1, R):
        s = (r + i) % R
        copy(lc.at[r], lc.at[r], ag_s, ag_r, (s, c)).start()

    cp_d.wait()
    inv_v[...] = invert_lower(d_v[...])

    wait(flip_in.at[pl.ds(0, R - 1)], fl_r)
    flip_in[r] = flip_v[r]
    total_flip = flip_in[0]
    for i in range(1, R):
        total_flip = total_flip + flip_in[i]
    route_src[...] = total_flip

    @pl.when(jnp.logical_not(to_self))
    def _():
        copy(route_src, route_in, rt_s, rt_r, dev(to_r, to_z, to_k)).start()

    wait(lc.at[pl.ds(0, R - 1)], ag_r)
    weights = lc[...].reshape(4 * BLK, BLK)

    def direct_half(base):
        stacked = jnp.concatenate(
            [
                jnp.concatenate(
                    [s_v[base + a, pl.ds(b, BLK, stride=4), :] for b in range(4)], axis=1
                )
                for a in range(4)
            ],
            axis=0,
        )
        return dot(stacked, weights).reshape(HALF, SL, BLK)

    give_v[...] = direct_half((1 - k) * 4)
    pair = copy(give_v, pair_in, pr_s, pr_r, dev(r, z, 1 - k))
    pair.start()
    half_v[...] = direct_half(k * 4)
    own_sum = dot(
        pt_v[:, pl.ds(pl.multiple_of(k * 4 * BLK, BLK), 4 * BLK)], half_v[...].reshape(4 * BLK, BLK)
    ) + dot(
        pt_v[:, pl.ds(pl.multiple_of((1 - k) * 4 * BLK, BLK), 4 * BLK)],
        give_v[...].reshape(4 * BLK, BLK),
    )
    pair.wait()
    half_v[...] = half_v[...] + pair_in[...]

    def slice_for(delta):
        return slice_in_half(offset_of(r, (z + delta + Z) % Z))

    def chip(delta):
        return dev(r, (z + delta + Z) % Z, k)

    for d in range(2 * W, W, -1):
        copy(half_v.at[slice_for(d)], agg_far.at[d - W - 1], rs_s, rs_r.at[0], chip(d - W)).start()
    for d in range(2 * W - 1, W, -1):
        copy(half_v.at[slice_for(-d)], agg_near.at[d - W - 1], rs_s, rs_r.at[1], chip(W - d)).start()
    for d in range(W - 1, 0, -1):
        copy(half_v.at[slice_for(d)], fin_in.at[d - 1], rs_s, rs_r.at[2], chip(d)).start()
        copy(half_v.at[slice_for(-d)], fin_in.at[W - 1 + d - 1], rs_s, rs_r.at[2], chip(-d)).start()

    cp_b.wait()
    prod = dot_t(b_v[...], p_v[sid]) - own_sum - own_sum.T
    GL = BLK // R
    prod_v[...] = prod.reshape(R, GL, BLK)
    for i in range(1, R):
        s = (r + i) % R
        copy(prod_v.at[s], prod_in.at[r], g_s.at[0], g_r.at[0], (s, c)).start()

    wait(agg_far, rs_r.at[0])
    far = half_v[slice_for(W)]
    for i in range(W):
        far = far + agg_far[i]
    agg_out[0] = far
    copy(agg_out.at[0], fin_in.at[2 * W - 2], rs_s, rs_r.at[2], chip(W)).start()
    near = half_v[slice_for(-W)]
    if W > 1:
        wait(agg_near.at[pl.ds(0, W - 1)], rs_r.at[1])
        for i in range(W - 1):
            near = near + agg_near[i]
    agg_out[1] = near
    copy(agg_out.at[1], fin_in.at[2 * W - 1], rs_s, rs_r.at[2], chip(-W)).start()

    wait(prod_in.at[pl.ds(0, R - 1)], g_r.at[0])
    prod_in[r] = prod_v[r]
    acc = prod_in[0]
    for i in range(1, R):
        acc = acc + prod_in[i]
    psum_v[...] = acc
    for i in range(1, Z):
        copy(psum_v, psum_in.at[z], g_s.at[1], g_r.at[1], chip(i)).start()

    @pl.when(jnp.logical_not(to_self))
    def _():
        wait(route_in, rt_r)

    @pl.when(to_self)
    def _():
        route_in[...] = route_src[...]

    wait(fin_in, rs_r.at[2])
    total = half_v[my_slice]
    for i in range(2 * W):
        total = total + fin_in[i]
    total = b_v[...] - (total + route_in[...])
    x_v[sid] = dot(total, inv_v[...])

    def sid_at(delta):
        return k * HALF + slice_for(delta)

    def forward(s):
        copy(x_v.at[s], x_v.at[s], xp_s, xp_r, dev(r, z, 1 - k)).start()

    for d in range(W, 0, -1):
        copy(x_v.at[sid], x_v.at[sid], x_s, x_r.at[d], chip(d)).start()
        copy(x_v.at[sid], x_v.at[sid], x_s, x_r.at[2 * W + d], chip(-d)).start()
    forward(sid)
    far_sid = sid_at(-W)
    wait(x_v.at[far_sid], x_r.at[W])
    for d in range(W, 0, -1):
        copy(x_v.at[far_sid], x_v.at[far_sid], x_s, x_r.at[W + d], chip(d)).start()
    near_sid = sid_at(W)
    wait(x_v.at[near_sid], x_r.at[3 * W])
    for d in range(W - 1, 0, -1):
        copy(x_v.at[near_sid], x_v.at[near_sid], x_s, x_r.at[3 * W + d], chip(-d)).start()
    forward(far_sid)
    forward(near_sid)
    for d in range(1, W):
        wait(x_v.at[sid_at(-d)], x_r.at[d])
        forward(sid_at(-d))
        wait(x_v.at[sid_at(d)], x_r.at[2 * W + d])
        forward(sid_at(d))

    wait(psum_in.at[pl.ds(0, Z - 1)], g_r.at[1])
    psum_in[z] = psum_v[...]
    acc = psum_in[0]
    for i in range(1, Z):
        acc = acc + psum_in[i]
    ppair_v[...] = acc
    hand = copy(ppair_v, ppair_in, g_s.at[2], g_r.at[2], dev(r, z, 1 - k))
    hand.start()
    hand.wait()
    pfull_v[r] = ppair_v[...] + ppair_in[...]
    for i in range(1, R):
        copy(pfull_v.at[r], pfull_v.at[r], g_s.at[3], g_r.at[3], ((r + i) % R, c)).start()

    for d in range(1, W):
        wait(x_v.at[sid_at(-W - d)], x_r.at[W + d])
        forward(sid_at(-W - d))
        wait(x_v.at[sid_at(W + d)], x_r.at[3 * W + d])
        forward(sid_at(W + d))
    wait(x_v.at[sid_at(-2 * W)], x_r.at[2 * W])
    forward(sid_at(-2 * W))

    wait(pfull_v.at[pl.ds(0, R - 1)], g_r.at[3])
    full = pfull_v[...].reshape(BLK, BLK)
    gram = -dot_t(inv_v[...], full)
    row = lax.broadcasted_iota(jnp.int32, (BLK, BLK), 0)
    col = lax.broadcasted_iota(jnp.int32, (BLK, BLK), 1)
    gram_v[...] = jnp.where(row >= col, gram, jnp.zeros_like(gram))
    out_g = pltpu.make_async_copy(gram_v, g_out, loc.at[13])
    out_g.start()

    wait(x_v.at[pl.ds(0, HALF)], xp_r)
    out_x = pltpu.make_async_copy(x_v, x_out, loc.at[12])
    out_x.start()

    @pl.when(own)
    def _():
        wait(lc.at[pl.ds(0, R - 1)], sc_s)

    wait(lc.at[pl.ds(0, R - 1)], ag_s)
    wait(flip_in.at[pl.ds(0, R - 1)], fl_s)

    @pl.when(jnp.logical_not(to_self))
    def _():
        wait(route_src, rt_s)

    wait(half_v.at[pl.ds(0, Z - 1)], rs_s)
    wait(half_v.at[pl.ds(0, Z - 1)], x_s)
    wait(half_v, xp_s)
    wait(prod_in.at[pl.ds(0, R - 1)], g_s.at[0])
    wait(psum_in.at[pl.ds(0, Z - 1)], g_s.at[1])
    wait(pfull_v.at[pl.ds(0, R - 1)], g_s.at[3])
    out_g.wait()
    out_x.wait()


def solution(mesh):
    R, C = mesh.shape["row"], mesh.shape["col"]
    Z = C // 2
    W = Z // 4
    SL = 8 * BLK // C
    NS = BLK // SL
    HALF = 4 * NS
    GL = BLK // R

    def per_device(trail_adjoint, panel, panel_adjoint, diag_block):
        any_spec = pl.BlockSpec(memory_space=pl.ANY)
        vm = lambda *shape: pltpu.VMEM(shape, F32)
        dma = pltpu.SemaphoreType.DMA
        x, gram = pl.pallas_call(
            functools.partial(kernel, R, C),
            out_shape=(
                jax.ShapeDtypeStruct((2 * HALF, SL, BLK), F32),
                jax.ShapeDtypeStruct((BLK, BLK), F32),
            ),
            in_specs=[any_spec] * 4,
            out_specs=(any_spec, any_spec),
            scratch_shapes=[
                vm(8, 4 * BLK, BLK),
                vm(2 * HALF, SL, BLK),
                vm(SL, BLK),
                vm(BLK, BLK),
                vm(BLK, 8 * BLK),
                vm(BLK, BLK),
                vm(R, SL, BLK),
                vm(R, SL, BLK),
                vm(R, SL, BLK),
                vm(SL, BLK),
                vm(SL, BLK),
                vm(HALF, SL, BLK),
                vm(HALF, SL, BLK),
                vm(HALF, SL, BLK),
                vm(W, SL, BLK),
                vm(max(W - 1, 1), SL, BLK),
                vm(2, SL, BLK),
                vm(2 * W, SL, BLK),
                vm(2 * HALF, SL, BLK),
                vm(R, GL, BLK),
                vm(R, GL, BLK),
                vm(GL, BLK),
                vm(Z, GL, BLK),
                vm(GL, BLK),
                vm(GL, BLK),
                vm(R, GL, BLK),
                vm(BLK, BLK),
                dma((14,)),
                dma(()),
                dma(()),
                dma(()),
                dma(()),
                dma(()),
                dma(()),
                dma(()),
                dma(()),
                dma(()),
                dma(()),
                dma(()),
                dma((3,)),
                dma(()),
                dma((4 * W + 1,)),
                dma(()),
                dma(()),
                dma((4,)),
                dma((4,)),
            ],
            compiler_params=pltpu.CompilerParams(
                collective_id=0, has_side_effects=True, vmem_limit_bytes=32 * 1024 * 1024
            ),
        )(
            trail_adjoint.reshape(8, 4 * BLK, BLK),
            panel.reshape(2 * HALF, SL, BLK),
            panel_adjoint.reshape(2 * HALF, SL, BLK),
            diag_block,
        )
        return x.reshape(8, BLK, BLK), gram

    return jax.shard_map(
        per_device,
        mesh=mesh,
        in_specs=(P(None, "row", None, "col"), P(None, "row", None), P(None, "row", None), P()),
        out_specs=(P(None, "row", None), P()),
        check_vma=False,
    )
```

```python
import functools

import jax
import jax.numpy as jnp
from jax import lax
from jax.experimental import pallas as pl
from jax.experimental.pallas import tpu as pltpu
from jax.sharding import PartitionSpec as P

MESH = pl.DeviceIdType.MESH
F32 = jnp.float32
BF16 = jnp.bfloat16
HI = lax.Precision.HIGHEST
BLK = 128


def dot(a, b):
    return jnp.dot(a, b, precision=HI, preferred_element_type=F32)


def dot_t(a, b):
    return lax.dot_general(
        a, b, (((0,), (0,)), ((), ())), precision=HI, preferred_element_type=F32
    )


def invert_lower(d):
    n = d.shape[0]
    row = lax.broadcasted_iota(jnp.int32, (n, n), 0)
    col = lax.broadcasted_iota(jnp.int32, (n, n), 1)
    eye = row == col
    zero = jnp.zeros_like(d)
    diag = jnp.where(eye, d, zero)
    recip_row = 1.0 / jnp.sum(diag, axis=1, keepdims=True)
    recip_col = 1.0 / jnp.sum(diag, axis=0, keepdims=True)

    def below(shift):
        same = lax.shift_right_logical(row, shift + 1) == lax.shift_right_logical(col, shift + 1)
        other = lax.shift_right_logical(row, shift) != lax.shift_right_logical(col, shift)
        return jnp.where(same & other & (row > col), d, zero)

    inv = jnp.where(eye, jnp.broadcast_to(recip_row, (n, n)), -(below(0) * recip_row) * recip_col)
    shift = 1
    while (1 << shift) < n:
        inv = inv - dot(inv, dot(below(shift), inv))
        shift += 1
    return inv


def split(x):
    hi = x.astype(BF16)
    return hi, (x - hi.astype(F32)).astype(BF16)


def bdot(a, b):
    return jnp.dot(a, b, preferred_element_type=F32)


def kernel(
    rows,
    cols,
    s_hbm,
    panel_hbm,
    given_hbm,
    diag_hbm,
    x_v,
    g_out,
    s_v,
    s_hi,
    s_lo,
    p_v,
    b_v,
    d_v,
    pt_v,
    inv_v,
    lc,
    flip_v,
    flip_in,
    route_src,
    route_in,
    half_v,
    give_v,
    pair_in,
    agg_far,
    agg_near,
    agg_out,
    fin_in,
    prod_v,
    prod_in,
    quad_v,
    quad_in,
    cross_v,
    cross_in,
    ppair_v,
    ppair_in,
    pfull_v,
    loc,
    sc_s,
    sc_r,
    ag_s,
    ag_r,
    fl_s,
    fl_r,
    rt_s,
    rt_r,
    pr_s,
    pr_r,
    rs_s,
    rs_r,
    x_s,
    x_r,
    xp_s,
    xp_r,
    g_s,
    g_r,
):
    R, C = rows, cols
    Z = C // 2
    W = Z // 4
    SL = 8 * BLK // C
    NS = BLK // SL
    HALF = 4 * NS
    HR = 4 * BLK
    r = lax.axis_index("row")
    c = lax.axis_index("col")
    z = c // 2
    k = c % 2

    def dev(row, chip, core):
        return (row, chip * 2 + core)

    def plane(i):
        return ((r + i) & (R - 1), c)

    def chip(delta):
        return dev(r, (z + delta) & (Z - 1), k)

    def copy(src, dst, send, recv, device):
        return pltpu.make_async_remote_copy(
            src_ref=src,
            dst_ref=dst,
            send_sem=send,
            recv_sem=recv,
            device_id=device,
            device_id_type=MESH,
        )

    def wait(ref, sem):
        pltpu.make_async_copy(ref, ref, sem).wait()

    def offset_of(row, at):
        return (at - row // 2 + R // 4) & (Z - 1)

    def slice_in_half(o):
        m = o & (R // 2 - 1)
        return (2 * (m // NS) + o // (R // 2)) * NS + (m & (NS - 1))

    def slice_for(delta):
        return slice_in_half(offset_of(r, (z + delta) & (Z - 1)))

    barrier = pltpu.get_barrier_semaphore()
    other = dev(r, z, 1 - k)
    for i in range(1, R):
        pl.semaphore_signal(barrier, inc=1, device_id=plane(i), device_id_type=MESH)
    for i in range(1, W + 1):
        for delta in (i, -i):
            for core in (0, 1):
                near_by = dev(r, (z + delta) & (Z - 1), core)
                pl.semaphore_signal(barrier, inc=1, device_id=near_by, device_id_type=MESH)
    pl.semaphore_signal(barrier, inc=1, device_id=other, device_id_type=MESH)

    cp_s = [pltpu.make_async_copy(s_hbm.at[a], s_v.at[a], loc.at[1 + a]) for a in range(8)]
    cp_panel = pltpu.make_async_copy(panel_hbm, p_v, loc.at[0])
    for one in cp_s:
        one.start()
    cp_panel.start()
    my_slice = slice_for(0)
    sid = k * HALF + my_slice
    cp_b = pltpu.make_async_copy(given_hbm.at[sid], b_v, loc.at[9])
    cp_b.start()
    cp_d = pltpu.make_async_copy(diag_hbm, d_v, loc.at[10])
    cp_d.start()

    pl.semaphore_wait(barrier, R - 1 + 4 * W + 1)

    owner = c & (R - 1)
    which = c // R
    own = owner == r

    def piece(s):
        return panel_hbm.at[(2 * (s // NS) + which) * NS + (s & (NS - 1))]

    @pl.when(own)
    def _():
        for i in range(1, R):
            s = (r + i) & (R - 1)
            copy(piece(s), lc.at[s], sc_s, sc_r, plane(i)).start()
        mine = pltpu.make_async_copy(piece(r), lc.at[r], loc.at[11])
        mine.start()
        mine.wait()

    for a in range(8):
        cp_s[a].wait()

        for b in range(4):
            hi, lo = split(s_v[a, pl.ds(b, BLK, stride=4), :])
            s_hi[pl.ds(a * BLK, BLK), pl.ds(b * BLK, BLK)] = hi
            s_lo[pl.ds(a * BLK, BLK), pl.ds(b * BLK, BLK)] = lo
    cp_panel.wait()
    for a in range(8):
        hi, lo = split(p_v[pl.ds(a * NS, NS)].reshape(BLK, BLK).T)
        pt_v[pl.ds(0, BLK), pl.ds(a * BLK, BLK)] = hi
        pt_v[pl.ds(BLK, BLK), pl.ds(a * BLK, BLK)] = lo
    for b in range(2):
        wide = pl.ds(b * 2 * BLK, 2 * BLK)
        both = bdot(pt_v[...], s_hi[:, wide])
        part = both[:BLK] + (both[BLK:] + bdot(pt_v[pl.ds(0, BLK), :], s_lo[:, wide]))
        flip_v[pl.ds(b * 2 * NS, 2 * NS)] = part.T.reshape(2 * NS, SL, BLK)
    for i in range(1, R):
        copy(flip_v.at[(r + i) & (R - 1)], flip_in.at[r], fl_s, fl_r, plane(i)).start()

    @pl.when(jnp.logical_not(own))
    def _():
        wait(lc.at[r], sc_r)

    for i in range(1, R):
        copy(lc.at[r], lc.at[r], ag_s, ag_r, plane(i)).start()

    cp_d.wait()
    inv_v[...] = invert_lower(d_v[...])

    wait(flip_in.at[pl.ds(0, R - 1)], fl_r)
    flip_in[r] = flip_v[r]
    total_flip = flip_in[0]
    for i in range(1, R):
        total_flip = total_flip + flip_in[i]
    route_src[...] = total_flip

    wait(lc.at[pl.ds(0, R - 1)], ag_r)

    to_r = owner
    to_z = (z - R // 4 + (r & (R // 2 - 1))) & (Z - 1)
    to_k = r // (R // 2)
    to_self = (to_r == r) & (to_z == z) & (to_k == k)

    @pl.when(jnp.logical_not(to_self))
    def _():
        copy(route_src, route_in, rt_s, rt_r, dev(to_r, to_z, to_k)).start()

    @pl.when(to_self)
    def _():
        route_in[...] = route_src[...]

    w_hi, w_lo = split(lc[...].reshape(HR, BLK))
    w_both = jnp.concatenate([w_hi, w_lo], axis=1)

    def direct_half(base):
        at = pl.ds(pl.multiple_of(base * HR, HR), HR)
        both = bdot(s_hi[at, :], w_both)
        out = both[:, :BLK] + (both[:, BLK:] + bdot(s_lo[at, :], w_hi))
        return out.reshape(HALF, SL, BLK)

    give_v[...] = direct_half(1 - k)
    pair = copy(give_v, pair_in, pr_s, pr_r, other)
    pair.start()
    kept = direct_half(k)
    kept_hi, kept_lo = split(kept.reshape(HR, BLK))
    pair.wait()
    half_v[...] = kept + pair_in[...]

    for d in range(2 * W, W, -1):
        copy(half_v.at[slice_for(d)], agg_far.at[d - W - 1], rs_s, rs_r.at[0], chip(d - W)).start()
        if d < 2 * W:
            copy(
                half_v.at[slice_for(-d)], agg_near.at[d - W - 1], rs_s, rs_r.at[1], chip(W - d)
            ).start()
    for d in range(W - 1, 0, -1):
        copy(half_v.at[slice_for(d)], fin_in.at[d - 1], rs_s, rs_r.at[2], chip(d)).start()
        copy(half_v.at[slice_for(-d)], fin_in.at[W + d - 2], rs_s, rs_r.at[2], chip(-d)).start()

    def product(base, hi, lo):
        at = pl.ds(pl.multiple_of(base * HR, HR), HR)
        both = bdot(pt_v[:, at], hi)
        return both[:BLK] + (both[BLK:] + bdot(pt_v[pl.ds(0, BLK), at], lo))

    give_hi, give_lo = split(give_v[...].reshape(HR, BLK))
    own_sum = product(k, kept_hi, kept_lo) + product(1 - k, give_hi, give_lo)
    cp_b.wait()
    prod = dot_t(b_v[...], p_v[sid]) - (own_sum + own_sum.T)
    prod_v[...] = prod.reshape(R, BLK // R, BLK)
    for i in range(1, R):
        copy(prod_v.at[(r + i) & (R - 1)], prod_in.at[r], g_s.at[0], g_r.at[0], plane(i)).start()

    wait(agg_far, rs_r.at[0])
    far = half_v[slice_for(W)]
    for i in range(W):
        far = far + agg_far[i]
    agg_out[0] = far
    copy(agg_out.at[0], fin_in.at[2 * W - 2], rs_s, rs_r.at[2], chip(W)).start()
    near = half_v[slice_for(-W)]
    if W > 1:
        wait(agg_near.at[pl.ds(0, W - 1)], rs_r.at[1])
        for i in range(W - 1):
            near = near + agg_near[i]
    agg_out[1] = near
    copy(agg_out.at[1], fin_in.at[2 * W - 1], rs_s, rs_r.at[2], chip(-W)).start()

    wait(prod_in.at[pl.ds(0, R - 1)], g_r.at[0])
    prod_in[r] = prod_v[r]
    acc = prod_in[0]
    for i in range(1, R):
        acc = acc + prod_in[i]
    group, lane = z // W, z & (W - 1)
    quad_v[...] = acc
    for i in range(1, W):
        mate = dev(r, group * W + ((lane + i) & (W - 1)), k)
        copy(quad_v, quad_in.at[lane], g_s.at[1], g_r.at[1], mate).start()

    @pl.when(jnp.logical_not(to_self))
    def _():
        wait(route_in, rt_r)

    wait(fin_in, rs_r.at[2])
    total = half_v[my_slice]
    for i in range(2 * W):
        total = total + fin_in[i]
    total = b_v[...] - (total + route_in[...])
    x_v[sid] = dot(total, inv_v[...])

    def sid_at(delta):
        return k * HALF + slice_for(delta)

    def send_x(s, sem, device):
        copy(x_v.at[s], x_v.at[s], x_s, x_r.at[sem], device).start()

    def forward(s):
        copy(x_v.at[s], x_v.at[s], xp_s, xp_r, other).start()

    for d in range(W, 0, -1):
        send_x(sid, d, chip(d))
        send_x(sid, 2 * W + d, chip(-d))
    forward(sid)

    if W > 1:
        wait(quad_in.at[pl.ds(0, W - 1)], g_r.at[1])
    quad_in[lane] = quad_v[...]
    acc = quad_in[0]
    for i in range(1, W):
        acc = acc + quad_in[i]
    cross_v[...] = acc
    for i in range(1, 4):
        copy(cross_v, cross_in.at[group], g_s.at[2], g_r.at[2], chip(i * W)).start()

    far_sid = sid_at(-W)
    wait(x_v.at[far_sid], x_r.at[W])
    for d in range(W, 0, -1):
        send_x(far_sid, W + d, chip(d))
    near_sid = sid_at(W)
    wait(x_v.at[near_sid], x_r.at[3 * W])
    for d in range(W - 1, 0, -1):
        send_x(near_sid, 3 * W + d, chip(-d))
    forward(far_sid)
    forward(near_sid)
    for d in range(1, W):
        wait(x_v.at[sid_at(-d)], x_r.at[d])
        forward(sid_at(-d))
        wait(x_v.at[sid_at(d)], x_r.at[2 * W + d])
        forward(sid_at(d))

    wait(cross_in.at[pl.ds(0, 3)], g_r.at[2])
    cross_in[group] = cross_v[...]
    ppair_v[...] = (cross_in[0] + cross_in[1]) + (cross_in[2] + cross_in[3])
    hand = copy(ppair_v, ppair_in, g_s.at[3], g_r.at[3], other)
    hand.start()
    hand.wait()
    pfull_v[r] = ppair_v[...] + ppair_in[...]
    for i in range(1, R):
        copy(pfull_v.at[r], pfull_v.at[r], g_s.at[4], g_r.at[4], plane(i)).start()

    for d in range(1, W):
        wait(x_v.at[sid_at(-W - d)], x_r.at[W + d])
        forward(sid_at(-W - d))
        wait(x_v.at[sid_at(W + d)], x_r.at[3 * W + d])
        forward(sid_at(W + d))
    wait(x_v.at[sid_at(-2 * W)], x_r.at[2 * W])
    forward(sid_at(-2 * W))

    wait(pfull_v.at[pl.ds(0, R - 1)], g_r.at[4])
    gram = -dot_t(inv_v[...], pfull_v[...].reshape(BLK, BLK))
    row = lax.broadcasted_iota(jnp.int32, (BLK, BLK), 0)
    col = lax.broadcasted_iota(jnp.int32, (BLK, BLK), 1)
    g_out[...] = jnp.where(row >= col, gram, jnp.zeros_like(gram))

    @pl.when(own)
    def _():
        wait(lc.at[pl.ds(0, R - 1)], sc_s)

    wait(lc.at[pl.ds(0, R - 1)], ag_s)
    wait(flip_in.at[pl.ds(0, R - 1)], fl_s)

    @pl.when(jnp.logical_not(to_self))
    def _():
        wait(route_src, rt_s)

    wait(half_v.at[pl.ds(0, Z - 1)], rs_s)
    wait(half_v.at[pl.ds(0, Z - 1)], x_s)
    wait(prod_in.at[pl.ds(0, R - 1)], g_s.at[0])
    if W > 1:
        wait(quad_in.at[pl.ds(0, W - 1)], g_s.at[1])
    wait(cross_in.at[pl.ds(0, 3)], g_s.at[2])
    wait(pfull_v.at[pl.ds(0, R - 1)], g_s.at[4])
    wait(half_v, xp_s)
    wait(half_v, xp_r)


def solution(mesh):
    R, C = mesh.shape["row"], mesh.shape["col"]
    Z = C // 2
    W = Z // 4
    SL = 8 * BLK // C
    NS = BLK // SL
    HALF = 4 * NS
    GL = BLK // R

    def per_device(trail_adjoint, panel, panel_adjoint, diag_block):
        hbm = pl.BlockSpec(memory_space=pltpu.MemorySpace.HBM)
        vmem = pl.BlockSpec(memory_space=pltpu.MemorySpace.VMEM)
        vm = lambda *shape: pltpu.VMEM(shape, F32)
        dma = pltpu.SemaphoreType.DMA
        in_hbm = lambda x: pltpu.with_memory_space_constraint(x, pltpu.MemorySpace.HBM)
        x, gram = pl.pallas_call(
            functools.partial(kernel, R, C),
            out_shape=(
                jax.ShapeDtypeStruct((2 * HALF, SL, BLK), F32),
                jax.ShapeDtypeStruct((BLK, BLK), F32),
            ),
            in_specs=[hbm] * 4,
            out_specs=(vmem, vmem),
            scratch_shapes=[
                vm(8, 4 * BLK, BLK),
                pltpu.VMEM((8 * BLK, 4 * BLK), BF16),
                pltpu.VMEM((8 * BLK, 4 * BLK), BF16),
                vm(2 * HALF, SL, BLK),
                vm(SL, BLK),
                vm(BLK, BLK),
                pltpu.VMEM((2 * BLK, 8 * BLK), BF16),
                vm(BLK, BLK),
                vm(R, SL, BLK),
                vm(R, SL, BLK),
                vm(R, SL, BLK),
                vm(SL, BLK),
                vm(SL, BLK),
                vm(HALF, SL, BLK),
                vm(HALF, SL, BLK),
                vm(HALF, SL, BLK),
                vm(W, SL, BLK),
                vm(max(W - 1, 1), SL, BLK),
                vm(2, SL, BLK),
                vm(2 * W, SL, BLK),
                vm(R, GL, BLK),
                vm(R, GL, BLK),
                vm(GL, BLK),
                vm(W, GL, BLK),
                vm(GL, BLK),
                vm(4, GL, BLK),
                vm(GL, BLK),
                vm(GL, BLK),
                vm(R, GL, BLK),
                dma((12,)),
                dma(()),
                dma(()),
                dma(()),
                dma(()),
                dma(()),
                dma(()),
                dma(()),
                dma(()),
                dma(()),
                dma(()),
                dma(()),
                dma((3,)),
                dma(()),
                dma((4 * W,)),
                dma(()),
                dma(()),
                dma((5,)),
                dma((5,)),
            ],
            compiler_params=pltpu.CompilerParams(
                collective_id=0, has_side_effects=True, vmem_limit_bytes=32 * 1024 * 1024
            ),
        )(
            in_hbm(trail_adjoint.reshape(8, 4 * BLK, BLK)),
            in_hbm(panel.reshape(2 * HALF, SL, BLK)),
            in_hbm(panel_adjoint.reshape(2 * HALF, SL, BLK)),
            in_hbm(diag_block),
        )
        return x.reshape(8, BLK, BLK), gram

    return jax.shard_map(
        per_device,
        mesh=mesh,
        in_specs=(P(None, "row", None, "col"), P(None, "row", None), P(None, "row", None), P()),
        out_specs=(P(None, "row", None), P()),
        check_vma=False,
    )
```

```python
import functools
import math

import jax
import jax.numpy as jnp
from jax import lax
from jax.experimental import pallas as pl
from jax.experimental.pallas import tpu as pltpu
from jax.sharding import PartitionSpec as P

MESH = pl.DeviceIdType.MESH
F32 = jnp.float32
BF16 = jnp.bfloat16
HI = lax.Precision.HIGHEST
BLK = 128
DELAY = 800


def dot(a, b):
    return jnp.dot(a, b, precision=HI, preferred_element_type=F32)


def dot_t(a, b):
    return lax.dot_general(
        a, b, (((0,), (0,)), ((), ())), precision=HI, preferred_element_type=F32
    )


def invert_lower(d):
    n = d.shape[0]
    row = lax.broadcasted_iota(jnp.int32, (n, n), 0)
    col = lax.broadcasted_iota(jnp.int32, (n, n), 1)
    eye = row == col
    zero = jnp.zeros_like(d)
    diag = jnp.where(eye, d, zero)
    recip_row = 1.0 / jnp.sum(diag, axis=1, keepdims=True)
    recip_col = 1.0 / jnp.sum(diag, axis=0, keepdims=True)

    def below(shift):
        same = lax.shift_right_logical(row, shift + 1) == lax.shift_right_logical(col, shift + 1)
        other = lax.shift_right_logical(row, shift) != lax.shift_right_logical(col, shift)
        return jnp.where(same & other & (row > col), d, zero)

    inv = jnp.where(eye, jnp.broadcast_to(recip_row, (n, n)), -(below(0) * recip_row) * recip_col)
    shift = 1
    while (1 << shift) < n:
        inv = inv - dot(inv, dot(below(shift), inv))
        shift += 1
    return inv


def split(x):
    hi = x.astype(BF16)
    return hi, (x - hi.astype(F32)).astype(BF16)


def bdot(a, b):
    return jnp.dot(a, b, preferred_element_type=F32)


def kernel(
    rows,
    cols,
    s_hbm,
    panel_hbm,
    given_hbm,
    diag_hbm,
    x_v,
    g_out,
    s_v,
    s_hi,
    s_lo,
    p_v,
    b_v,
    d_v,
    pt_v,
    inv_v,
    lc,
    flip_v,
    flip_in,
    route_src,
    route_in,
    half_v,
    give_v,
    pair_in,
    agg_far,
    agg_near,
    agg_out,
    fin_in,
    prod_v,
    prod_in,
    quad_v,
    quad_in,
    cross_v,
    cross_in,
    ppair_v,
    ppair_in,
    pfull_v,
    loc,
    sc_s,
    sc_r,
    ag_s,
    ag_r,
    fl_s,
    fl_r,
    rt_s,
    rt_r,
    pr_s,
    pr_r,
    rs_s,
    rs_r,
    x_s,
    x_r,
    xp_s,
    xp_r,
    g_s,
    g_r,
):
    R, C = rows, cols
    Z = C // 2
    W = Z // 4
    SL = 8 * BLK // C
    NS = BLK // SL
    HALF = 4 * NS
    HR = 4 * BLK
    side = math.isqrt(R)
    r = lax.axis_index("row")
    c = lax.axis_index("col")
    z = c // 2
    k = c % 2

    def dev(row, chip, core):
        return (row, chip * 2 + core)

    hops = lambda d: min(d, side - d)
    steps = [(dx, dy) for dx in range(side) for dy in range(side) if dx + dy > 0]
    steps.sort(key=lambda d: -(hops(d[0]) + hops(d[1])))

    def at(step):
        dx, dy = step
        return ((r // side + dx) & (side - 1)) * side + ((r + dy) & (side - 1))

    sign = 1 - 2 * k

    def away(delta):
        return (z + sign * delta) & (Z - 1)

    def chip(delta):
        return dev(r, away(delta), k)

    def copy(src, dst, send, recv, device):
        return pltpu.make_async_remote_copy(
            src_ref=src,
            dst_ref=dst,
            send_sem=send,
            recv_sem=recv,
            device_id=device,
            device_id_type=MESH,
        )

    def wait(ref, sem):
        pltpu.make_async_copy(ref, ref, sem).wait()

    def offset_of(row, at):
        return (at - row // 2 + R // 4) & (Z - 1)

    def slice_in_half(o):
        m = o & (R // 2 - 1)
        return (2 * (m // NS) + o // (R // 2)) * NS + (m & (NS - 1))

    def slice_for(delta):
        return slice_in_half(offset_of(r, away(delta)))

    barrier = pltpu.get_barrier_semaphore()
    other = dev(r, z, 1 - k)
    for step in steps:
        pl.semaphore_signal(barrier, inc=1, device_id=(at(step), c), device_id_type=MESH)
    for i in range(W, 0, -1):
        for delta in (i, -i):
            for core in (0, 1):
                near_by = dev(r, (z + delta) & (Z - 1), core)
                pl.semaphore_signal(barrier, inc=1, device_id=near_by, device_id_type=MESH)
    pl.semaphore_signal(barrier, inc=1, device_id=other, device_id_type=MESH)

    cp_s = [pltpu.make_async_copy(s_hbm.at[a], s_v.at[a], loc.at[1 + a]) for a in range(8)]
    cp_panel = pltpu.make_async_copy(panel_hbm, p_v, loc.at[0])
    for one in cp_s:
        one.start()
    cp_panel.start()
    my_slice = slice_for(0)
    sid = k * HALF + my_slice
    cp_b = pltpu.make_async_copy(given_hbm.at[sid], b_v, loc.at[9])
    cp_b.start()
    cp_d = pltpu.make_async_copy(diag_hbm, d_v, loc.at[10])
    cp_d.start()

    pl.semaphore_wait(barrier, R - 1 + 4 * W + 1)

    owner = c & (R - 1)
    which = c // R
    own = owner == r

    def piece(s):
        return panel_hbm.at[(2 * (s // NS) + which) * NS + (s & (NS - 1))]

    @pl.when(own)
    def _():
        for step in steps:
            s = at(step)
            copy(piece(s), lc.at[s], sc_s, sc_r, (s, c)).start()
        mine = pltpu.make_async_copy(piece(r), lc.at[r], loc.at[11])
        mine.start()
        mine.wait()

    for a in range(8):
        cp_s[a].wait()

        for b in range(4):
            hi, lo = split(s_v[a, pl.ds(b, BLK, stride=4), :])
            s_hi[pl.ds(a * BLK, BLK), pl.ds(b * BLK, BLK)] = hi
            s_lo[pl.ds(a * BLK, BLK), pl.ds(b * BLK, BLK)] = lo
    cp_panel.wait()
    for a in range(8):
        hi, lo = split(p_v[pl.ds(a * NS, NS)].reshape(BLK, BLK).T)
        pt_v[pl.ds(0, BLK), pl.ds(a * BLK, BLK)] = hi
        pt_v[pl.ds(BLK, BLK), pl.ds(a * BLK, BLK)] = lo
    for b in range(2):
        wide = pl.ds(b * 2 * BLK, 2 * BLK)
        both = bdot(pt_v[...], s_hi[:, wide])
        part = both[:BLK] + (both[BLK:] + bdot(pt_v[pl.ds(0, BLK), :], s_lo[:, wide]))
        flip_v[pl.ds(b * 2 * NS, 2 * NS)] = part.T.reshape(2 * NS, SL, BLK)
    for step in steps:
        copy(flip_v.at[at(step)], flip_in.at[r], fl_s, fl_r, (at(step), c)).start()

    @pl.when(jnp.logical_not(own))
    def _():
        wait(lc.at[r], sc_r)

    for step in steps:
        copy(lc.at[r], lc.at[r], ag_s, ag_r, (at(step), c)).start()

    cp_d.wait()
    inv_v[...] = invert_lower(d_v[...])

    wait(flip_in.at[pl.ds(0, R - 1)], fl_r)
    flip_in[r] = flip_v[r]
    total_flip = flip_in[0]
    for i in range(1, R):
        total_flip = total_flip + flip_in[i]
    route_src[...] = total_flip

    cross_part = dot_t(total_flip, lc[r])
    cp_b.wait()
    prod = dot_t(b_v[...], p_v[sid]) - (cross_part + cross_part.T)
    prod_v[...] = prod.reshape(R, BLK // R, BLK)
    for step in steps:
        copy(prod_v.at[at(step)], prod_in.at[r], g_s.at[0], g_r.at[0], (at(step), c)).start()

    wait(lc.at[pl.ds(0, R - 1)], ag_r)

    to_r = owner
    to_z = (z - R // 4 + (r & (R // 2 - 1))) & (Z - 1)
    to_k = r // (R // 2)
    to_self = (to_r == r) & (to_z == z) & (to_k == k)

    @pl.when(jnp.logical_not(to_self))
    def _():
        copy(route_src, route_in, rt_s, rt_r, dev(to_r, to_z, to_k)).start()

    @pl.when(to_self)
    def _():
        route_in[...] = route_src[...]

    w_hi, w_lo = split(lc[...].reshape(HR, BLK))
    w_both = jnp.concatenate([w_hi, w_lo], axis=1)

    def direct_half(base):
        at = pl.ds(pl.multiple_of(base * HR, HR), HR)
        both = bdot(s_hi[at, :], w_both)
        out = both[:, :BLK] + (both[:, BLK:] + bdot(s_lo[at, :], w_hi))
        return out.reshape(HALF, SL, BLK)

    give_v[...] = direct_half(1 - k)
    pair = copy(give_v, pair_in, pr_s, pr_r, other)
    pair.start()
    kept = direct_half(k)
    pair.wait()
    half_v[...] = kept + pair_in[...]

    for d in range(2 * W, W, -1):
        copy(half_v.at[slice_for(d)], agg_far.at[d - W - 1], rs_s, rs_r.at[0], chip(d - W)).start()
        if d < 2 * W:
            copy(
                half_v.at[slice_for(-d)], agg_near.at[d - W - 1], rs_s, rs_r.at[1], chip(W - d)
            ).start()

    wait(prod_in.at[pl.ds(0, R - 1)], g_r.at[0])
    prod_in[r] = prod_v[r]
    acc = prod_in[0]
    for i in range(1, R):
        acc = acc + prod_in[i]
    group, lane = z // W, z & (W - 1)
    quad_v[...] = acc
    for i in range(1, W):
        mate = dev(r, group * W + ((lane + i) & (W - 1)), k)
        copy(quad_v, quad_in.at[lane], g_s.at[1], g_r.at[1], mate).start()
    for d in range(W - 1, 0, -1):
        copy(half_v.at[slice_for(d)], fin_in.at[d - 1], rs_s, rs_r.at[2], chip(d)).start()
        copy(half_v.at[slice_for(-d)], fin_in.at[W + d - 2], rs_s, rs_r.at[2], chip(-d)).start()

    wait(agg_far, rs_r.at[0])
    far = half_v[slice_for(W)]
    for i in range(W):
        far = far + agg_far[i]
    agg_out[0] = far
    copy(agg_out.at[0], fin_in.at[2 * W - 2], rs_s, rs_r.at[2], chip(W)).start()
    near = half_v[slice_for(-W)]
    if W > 1:
        wait(agg_near.at[pl.ds(0, W - 1)], rs_r.at[1])
        for i in range(W - 1):
            near = near + agg_near[i]
    agg_out[1] = near
    copy(agg_out.at[1], fin_in.at[2 * W - 1], rs_s, rs_r.at[2], chip(-W)).start()

    if W > 1:
        wait(quad_in.at[pl.ds(0, W - 1)], g_r.at[1])
    quad_in[lane] = quad_v[...]
    acc = quad_in[0]
    for i in range(1, W):
        acc = acc + quad_in[i]
    cross_v[...] = acc
    for i in range(1, 4):
        copy(cross_v, cross_in.at[group], g_s.at[2], g_r.at[2], chip(i * W)).start()

    @pl.when(jnp.logical_not(to_self))
    def _():
        wait(route_in, rt_r)

    wait(fin_in, rs_r.at[2])
    total = half_v[my_slice]
    for i in range(2 * W):
        total = total + fin_in[i]
    total = b_v[...] - (total + route_in[...])
    x_v[sid] = dot(total, inv_v[...])

    def sid_at(delta):
        return k * HALF + slice_for(delta)

    def send_x(s, sem, device):
        copy(x_v.at[s], x_v.at[s], x_s, x_r.at[sem], device).start()

    def forward(s):
        copy(x_v.at[s], x_v.at[s], xp_s, xp_r, other).start()

    send_x(sid, W, chip(W))
    send_x(sid, 3 * W, chip(-W))
    forward(sid)
    pl.delay(DELAY)
    for d in range(W - 1, 0, -1):
        send_x(sid, d, chip(d))
        send_x(sid, 2 * W + d, chip(-d))

    far_sid = sid_at(-W)
    wait(x_v.at[far_sid], x_r.at[W])
    for d in range(W, 0, -1):
        send_x(far_sid, W + d, chip(d))
    near_sid = sid_at(W)
    wait(x_v.at[near_sid], x_r.at[3 * W])
    for d in range(W - 1, 0, -1):
        send_x(near_sid, 3 * W + d, chip(-d))
    forward(far_sid)
    forward(near_sid)
    for d in range(1, W):
        wait(x_v.at[sid_at(-d)], x_r.at[d])
        forward(sid_at(-d))
        wait(x_v.at[sid_at(d)], x_r.at[2 * W + d])
        forward(sid_at(d))

    wait(cross_in.at[pl.ds(0, 3)], g_r.at[2])
    cross_in[group] = cross_v[...]
    ppair_v[...] = (cross_in[0] + cross_in[1]) + (cross_in[2] + cross_in[3])
    hand = copy(ppair_v, ppair_in, g_s.at[3], g_r.at[3], other)
    hand.start()
    hand.wait()
    pfull_v[r] = ppair_v[...] + ppair_in[...]
    for step in steps:
        copy(pfull_v.at[r], pfull_v.at[r], g_s.at[4], g_r.at[4], (at(step), c)).start()

    for d in range(1, W):
        wait(x_v.at[sid_at(-W - d)], x_r.at[W + d])
        forward(sid_at(-W - d))
        wait(x_v.at[sid_at(W + d)], x_r.at[3 * W + d])
        forward(sid_at(W + d))
    wait(x_v.at[sid_at(-2 * W)], x_r.at[2 * W])
    forward(sid_at(-2 * W))

    wait(pfull_v.at[pl.ds(0, R - 1)], g_r.at[4])
    gram = -dot_t(inv_v[...], pfull_v[...].reshape(BLK, BLK))
    row = lax.broadcasted_iota(jnp.int32, (BLK, BLK), 0)
    col = lax.broadcasted_iota(jnp.int32, (BLK, BLK), 1)
    g_out[...] = jnp.where(row >= col, gram, jnp.zeros_like(gram))

    @pl.when(own)
    def _():
        wait(lc.at[pl.ds(0, R - 1)], sc_s)

    wait(lc.at[pl.ds(0, R - 1)], ag_s)
    wait(flip_in.at[pl.ds(0, R - 1)], fl_s)

    @pl.when(jnp.logical_not(to_self))
    def _():
        wait(route_src, rt_s)

    wait(half_v.at[pl.ds(0, Z - 1)], rs_s)
    wait(half_v.at[pl.ds(0, Z - 1)], x_s)
    wait(prod_in.at[pl.ds(0, R - 1)], g_s.at[0])
    if W > 1:
        wait(quad_in.at[pl.ds(0, W - 1)], g_s.at[1])
    wait(cross_in.at[pl.ds(0, 3)], g_s.at[2])
    wait(pfull_v.at[pl.ds(0, R - 1)], g_s.at[4])
    wait(half_v, xp_s)
    wait(half_v, xp_r)


def solution(mesh):
    R, C = mesh.shape["row"], mesh.shape["col"]
    Z = C // 2
    W = Z // 4
    SL = 8 * BLK // C
    NS = BLK // SL
    HALF = 4 * NS
    GL = BLK // R

    def per_device(trail_adjoint, panel, panel_adjoint, diag_block):
        hbm = pl.BlockSpec(memory_space=pltpu.MemorySpace.HBM)
        vmem = pl.BlockSpec(memory_space=pltpu.MemorySpace.VMEM)
        vm = lambda *shape: pltpu.VMEM(shape, F32)
        dma = pltpu.SemaphoreType.DMA
        in_hbm = lambda x: pltpu.with_memory_space_constraint(x, pltpu.MemorySpace.HBM)
        x, gram = pl.pallas_call(
            functools.partial(kernel, R, C),
            out_shape=(
                jax.ShapeDtypeStruct((2 * HALF, SL, BLK), F32),
                jax.ShapeDtypeStruct((BLK, BLK), F32),
            ),
            in_specs=[hbm] * 4,
            out_specs=(vmem, vmem),
            scratch_shapes=[
                vm(8, 4 * BLK, BLK),
                pltpu.VMEM((8 * BLK, 4 * BLK), BF16),
                pltpu.VMEM((8 * BLK, 4 * BLK), BF16),
                vm(2 * HALF, SL, BLK),
                vm(SL, BLK),
                vm(BLK, BLK),
                pltpu.VMEM((2 * BLK, 8 * BLK), BF16),
                vm(BLK, BLK),
                vm(R, SL, BLK),
                vm(R, SL, BLK),
                vm(R, SL, BLK),
                vm(SL, BLK),
                vm(SL, BLK),
                vm(HALF, SL, BLK),
                vm(HALF, SL, BLK),
                vm(HALF, SL, BLK),
                vm(W, SL, BLK),
                vm(max(W - 1, 1), SL, BLK),
                vm(2, SL, BLK),
                vm(2 * W, SL, BLK),
                vm(R, GL, BLK),
                vm(R, GL, BLK),
                vm(GL, BLK),
                vm(W, GL, BLK),
                vm(GL, BLK),
                vm(4, GL, BLK),
                vm(GL, BLK),
                vm(GL, BLK),
                vm(R, GL, BLK),
                dma((12,)),
                dma(()),
                dma(()),
                dma(()),
                dma(()),
                dma(()),
                dma(()),
                dma(()),
                dma(()),
                dma(()),
                dma(()),
                dma(()),
                dma((3,)),
                dma(()),
                dma((4 * W,)),
                dma(()),
                dma(()),
                dma((5,)),
                dma((5,)),
            ],
            compiler_params=pltpu.CompilerParams(
                collective_id=0, has_side_effects=True, vmem_limit_bytes=32 * 1024 * 1024
            ),
        )(
            in_hbm(trail_adjoint.reshape(8, 4 * BLK, BLK)),
            in_hbm(panel.reshape(2 * HALF, SL, BLK)),
            in_hbm(panel_adjoint.reshape(2 * HALF, SL, BLK)),
            in_hbm(diag_block),
        )
        return x.reshape(8, BLK, BLK), gram

    return jax.shard_map(
        per_device,
        mesh=mesh,
        in_specs=(P(None, "row", None, "col"), P(None, "row", None), P(None, "row", None), P()),
        out_specs=(P(None, "row", None), P()),
        check_vma=False,
    )
```

```python
import functools
import math

import jax
import jax.numpy as jnp
from jax import lax
from jax.experimental import pallas as pl
from jax.experimental.pallas import tpu as pltpu
from jax.sharding import PartitionSpec as P

MESH = pl.DeviceIdType.MESH
F32 = jnp.float32
BF16 = jnp.bfloat16
HI = lax.Precision.HIGHEST
BLK = 128
RS_PAUSE = 400
AG_PAUSE = 600


def dot(a, b):
    return jnp.dot(a, b, precision=HI, preferred_element_type=F32)


def dot_t(a, b):
    return lax.dot_general(
        a, b, (((0,), (0,)), ((), ())), precision=HI, preferred_element_type=F32
    )


def invert_lower(d):
    n = d.shape[0]
    row = lax.broadcasted_iota(jnp.int32, (n, n), 0)
    col = lax.broadcasted_iota(jnp.int32, (n, n), 1)
    eye = row == col
    zero = jnp.zeros_like(d)
    diag = jnp.where(eye, d, zero)
    recip_row = 1.0 / jnp.sum(diag, axis=1, keepdims=True)
    recip_col = 1.0 / jnp.sum(diag, axis=0, keepdims=True)

    def below(shift):
        same = lax.shift_right_logical(row, shift + 1) == lax.shift_right_logical(col, shift + 1)
        other = lax.shift_right_logical(row, shift) != lax.shift_right_logical(col, shift)
        return jnp.where(same & other & (row > col), d, zero)

    inv = jnp.where(eye, jnp.broadcast_to(recip_row, (n, n)), -(below(0) * recip_row) * recip_col)
    shift = 1
    while (1 << shift) < n:
        inv = inv - dot(inv, dot(below(shift), inv))
        shift += 1
    return inv


def split(x):
    hi = x.astype(BF16)
    return hi, (x - hi.astype(F32)).astype(BF16)


def bdot(a, b):
    return jnp.dot(a, b, preferred_element_type=F32)


def kernel(
    rows,
    cols,
    s_hbm,
    panel_hbm,
    given_hbm,
    diag_hbm,
    x_v,
    g_out,
    s_v,
    s_hi,
    s_lo,
    p_v,
    b_v,
    d_v,
    pt_v,
    inv_v,
    lc,
    flip_v,
    flip_in,
    route_src,
    route_in,
    half_v,
    give_v,
    pair_in,
    agg_far,
    agg_near,
    agg_out,
    fin_in,
    prod_v,
    prod_in,
    quad_v,
    quad_in,
    cross_v,
    cross_in,
    ppair_v,
    ppair_in,
    pfull_v,
    loc,
    sc_s,
    sc_r,
    ag_s,
    ag_r,
    fl_s,
    fl_r,
    rt_s,
    rt_r,
    pr_s,
    pr_r,
    rs_s,
    rs_r,
    x_s,
    x_r,
    xp_s,
    xp_r,
    g_s,
    g_r,
):
    R, C = rows, cols
    Z = C // 2
    W = Z // 4
    SL = 8 * BLK // C
    NS = BLK // SL
    HALF = 4 * NS
    HR = 4 * BLK
    side = math.isqrt(R)
    r = lax.axis_index("row")
    c = lax.axis_index("col")
    z = c // 2
    k = c % 2

    def dev(row, chip, core):
        return (row, chip * 2 + core)

    hops = lambda d: min(d, side - d)
    steps = [(dx, dy) for dx in range(side) for dy in range(side) if dx + dy > 0]
    steps.sort(key=lambda d: -(hops(d[0]) + hops(d[1])))

    def at(step):
        dx, dy = step
        return ((r // side + dx) & (side - 1)) * side + ((r + dy) & (side - 1))

    sign = 1 - 2 * k

    def away(delta):
        return (z + sign * delta) & (Z - 1)

    def chip(delta):
        return dev(r, away(delta), k)

    def copy(src, dst, send, recv, device):
        return pltpu.make_async_remote_copy(
            src_ref=src,
            dst_ref=dst,
            send_sem=send,
            recv_sem=recv,
            device_id=device,
            device_id_type=MESH,
        )

    def wait(ref, sem):
        pltpu.make_async_copy(ref, ref, sem).wait()

    def offset_of(row, at):
        return (at - row // 2 + R // 4) & (Z - 1)

    def slice_in_half(o):
        m = o & (R // 2 - 1)
        return (2 * (m // NS) + o // (R // 2)) * NS + (m & (NS - 1))

    def slice_for(delta):
        return slice_in_half(offset_of(r, away(delta)))

    barrier = pltpu.get_barrier_semaphore()
    other = dev(r, z, 1 - k)
    for step in steps:
        pl.semaphore_signal(barrier, inc=1, device_id=(at(step), c), device_id_type=MESH)
    for i in range(W, 0, -1):
        for delta in (i, -i):
            for core in (0, 1):
                near_by = dev(r, (z + delta) & (Z - 1), core)
                pl.semaphore_signal(barrier, inc=1, device_id=near_by, device_id_type=MESH)
    pl.semaphore_signal(barrier, inc=1, device_id=other, device_id_type=MESH)

    cp_s = [pltpu.make_async_copy(s_hbm.at[a], s_v.at[a], loc.at[1 + a]) for a in range(8)]
    cp_panel = pltpu.make_async_copy(panel_hbm, p_v, loc.at[0])
    for one in cp_s:
        one.start()
    cp_panel.start()
    my_slice = slice_for(0)
    sid = k * HALF + my_slice
    cp_b = pltpu.make_async_copy(given_hbm.at[sid], b_v, loc.at[9])
    cp_b.start()
    cp_d = pltpu.make_async_copy(diag_hbm, d_v, loc.at[10])
    cp_d.start()

    pl.semaphore_wait(barrier, R - 1 + 4 * W + 1)

    owner = c & (R - 1)
    which = c // R
    own = owner == r

    def piece(s):
        return panel_hbm.at[(2 * (s // NS) + which) * NS + (s & (NS - 1))]

    @pl.when(own)
    def _():
        for step in steps:
            s = at(step)
            copy(piece(s), lc.at[s], sc_s, sc_r, (s, c)).start()
        mine = pltpu.make_async_copy(piece(r), lc.at[r], loc.at[11])
        mine.start()
        mine.wait()

    for a in range(8):
        cp_s[a].wait()

        for b in range(4):
            hi, lo = split(s_v[a, pl.ds(b, BLK, stride=4), :])
            s_hi[pl.ds(a * BLK, BLK), pl.ds(b * BLK, BLK)] = hi
            s_lo[pl.ds(a * BLK, BLK), pl.ds(b * BLK, BLK)] = lo
    cp_panel.wait()
    for a in range(8):
        hi, lo = split(p_v[pl.ds(a * NS, NS)].reshape(BLK, BLK).T)
        pt_v[pl.ds(0, BLK), pl.ds(a * BLK, BLK)] = hi
        pt_v[pl.ds(BLK, BLK), pl.ds(a * BLK, BLK)] = lo
    for b in range(2):
        wide = pl.ds(b * 2 * BLK, 2 * BLK)
        both = bdot(pt_v[...], s_hi[:, wide])
        part = both[:BLK] + (both[BLK:] + bdot(pt_v[pl.ds(0, BLK), :], s_lo[:, wide]))
        flip_v[pl.ds(b * 2 * NS, 2 * NS)] = part.T.reshape(2 * NS, SL, BLK)
    for step in steps:
        copy(flip_v.at[at(step)], flip_in.at[r], fl_s, fl_r, (at(step), c)).start()

    @pl.when(jnp.logical_not(own))
    def _():
        wait(lc.at[r], sc_r)

    for step in steps:
        copy(lc.at[r], lc.at[r], ag_s, ag_r, (at(step), c)).start()

    cp_d.wait()
    inv_v[...] = invert_lower(d_v[...])

    wait(flip_in.at[pl.ds(0, R - 1)], fl_r)
    flip_in[r] = flip_v[r]
    total_flip = flip_in[0]
    for i in range(1, R):
        total_flip = total_flip + flip_in[i]
    route_src[...] = total_flip

    cross_part = dot_t(total_flip, lc[r])
    cp_b.wait()
    prod = dot_t(b_v[...], p_v[sid]) - (cross_part + cross_part.T)
    prod_v[...] = prod.reshape(R, BLK // R, BLK)
    for step in steps:
        copy(prod_v.at[at(step)], prod_in.at[r], g_s.at[0], g_r.at[0], (at(step), c)).start()

    wait(lc.at[pl.ds(0, R - 1)], ag_r)

    to_r = owner
    to_z = (z - R // 4 + (r & (R // 2 - 1))) & (Z - 1)
    to_k = r // (R // 2)
    to_self = (to_r == r) & (to_z == z) & (to_k == k)

    @pl.when(jnp.logical_not(to_self))
    def _():
        copy(route_src, route_in, rt_s, rt_r, dev(to_r, to_z, to_k)).start()

    @pl.when(to_self)
    def _():
        route_in[...] = route_src[...]

    w_hi, w_lo = split(lc[...].reshape(HR, BLK))
    w_both = jnp.concatenate([w_hi, w_lo], axis=1)

    def direct_half(base):
        at = pl.ds(pl.multiple_of(base * HR, HR), HR)
        both = bdot(s_hi[at, :], w_both)
        out = both[:, :BLK] + (both[:, BLK:] + bdot(s_lo[at, :], w_hi))
        return out.reshape(HALF, SL, BLK)

    give_v[...] = direct_half(1 - k)
    pair = copy(give_v, pair_in, pr_s, pr_r, other)
    pair.start()
    kept = direct_half(k)
    pair.wait()
    half_v[...] = kept + pair_in[...]

    for d in range(2 * W, W, -1):
        copy(half_v.at[slice_for(d)], agg_far.at[d - W - 1], rs_s, rs_r.at[0], chip(d - W)).start()
        if d < 2 * W:
            copy(
                half_v.at[slice_for(-d)], agg_near.at[d - W - 1], rs_s, rs_r.at[1], chip(W - d)
            ).start()

    pl.delay(RS_PAUSE)
    for d in range(W - 1, 0, -1):
        copy(half_v.at[slice_for(d)], fin_in.at[d - 1], rs_s, rs_r.at[2], chip(d)).start()
        copy(half_v.at[slice_for(-d)], fin_in.at[W + d - 2], rs_s, rs_r.at[2], chip(-d)).start()

    wait(prod_in.at[pl.ds(0, R - 1)], g_r.at[0])
    prod_in[r] = prod_v[r]
    acc = prod_in[0]
    for i in range(1, R):
        acc = acc + prod_in[i]
    group, lane = z // W, z & (W - 1)
    quad_v[...] = acc
    for i in range(1, W):
        mate = dev(r, group * W + ((lane + i) & (W - 1)), k)
        copy(quad_v, quad_in.at[lane], g_s.at[1], g_r.at[1], mate).start()

    wait(agg_far, rs_r.at[0])
    far = half_v[slice_for(W)]
    for i in range(W):
        far = far + agg_far[i]
    agg_out[0] = far
    copy(agg_out.at[0], fin_in.at[2 * W - 2], rs_s, rs_r.at[2], chip(W)).start()
    near = half_v[slice_for(-W)]
    if W > 1:
        wait(agg_near.at[pl.ds(0, W - 1)], rs_r.at[1])
        for i in range(W - 1):
            near = near + agg_near[i]
    agg_out[1] = near
    copy(agg_out.at[1], fin_in.at[2 * W - 1], rs_s, rs_r.at[2], chip(-W)).start()

    if W > 1:
        wait(quad_in.at[pl.ds(0, W - 1)], g_r.at[1])
    quad_in[lane] = quad_v[...]
    acc = quad_in[0]
    for i in range(1, W):
        acc = acc + quad_in[i]
    cross_v[...] = acc
    for i in range(1, 4):
        copy(cross_v, cross_in.at[group], g_s.at[2], g_r.at[2], chip(i * W)).start()

    @pl.when(jnp.logical_not(to_self))
    def _():
        wait(route_in, rt_r)

    wait(fin_in, rs_r.at[2])
    total = half_v[my_slice]
    for i in range(2 * W):
        total = total + fin_in[i]
    total = b_v[...] - (total + route_in[...])
    x_v[sid] = dot(total, inv_v[...])

    def sid_at(delta):
        return k * HALF + slice_for(delta)

    def send_x(s, sem, device):
        copy(x_v.at[s], x_v.at[s], x_s, x_r.at[sem], device).start()

    def forward(s):
        copy(x_v.at[s], x_v.at[s], xp_s, xp_r, other).start()

    send_x(sid, W, chip(W))
    send_x(sid, 3 * W, chip(-W))
    forward(sid)
    pl.delay(AG_PAUSE)
    for d in range(W - 1, 0, -1):
        send_x(sid, d, chip(d))
        send_x(sid, 2 * W + d, chip(-d))

    wait(cross_in.at[pl.ds(0, 3)], g_r.at[2])
    cross_in[group] = cross_v[...]
    ppair_v[...] = (cross_in[0] + cross_in[1]) + (cross_in[2] + cross_in[3])
    hand = copy(ppair_v, ppair_in, g_s.at[3], g_r.at[3], other)
    hand.start()

    far_sid = sid_at(-W)
    wait(x_v.at[far_sid], x_r.at[W])
    for d in range(W, 0, -1):
        send_x(far_sid, W + d, chip(d))
    near_sid = sid_at(W)
    wait(x_v.at[near_sid], x_r.at[3 * W])
    for d in range(W - 1, 0, -1):
        send_x(near_sid, 3 * W + d, chip(-d))
    hand.wait()
    pfull_v[r] = ppair_v[...] + ppair_in[...]
    for step in steps:
        copy(pfull_v.at[r], pfull_v.at[r], g_s.at[4], g_r.at[4], (at(step), c)).start()

    forward(far_sid)
    forward(near_sid)
    for d in range(1, W):
        wait(x_v.at[sid_at(-d)], x_r.at[d])
        forward(sid_at(-d))
        wait(x_v.at[sid_at(d)], x_r.at[2 * W + d])
        forward(sid_at(d))

    for d in range(1, W):
        wait(x_v.at[sid_at(-W - d)], x_r.at[W + d])
        forward(sid_at(-W - d))
        wait(x_v.at[sid_at(W + d)], x_r.at[3 * W + d])
        forward(sid_at(W + d))
    wait(x_v.at[sid_at(-2 * W)], x_r.at[2 * W])
    forward(sid_at(-2 * W))

    wait(pfull_v.at[pl.ds(0, R - 1)], g_r.at[4])
    gram = -dot_t(inv_v[...], pfull_v[...].reshape(BLK, BLK))
    row = lax.broadcasted_iota(jnp.int32, (BLK, BLK), 0)
    col = lax.broadcasted_iota(jnp.int32, (BLK, BLK), 1)
    g_out[...] = jnp.where(row >= col, gram, jnp.zeros_like(gram))

    @pl.when(own)
    def _():
        wait(lc.at[pl.ds(0, R - 1)], sc_s)

    wait(lc.at[pl.ds(0, R - 1)], ag_s)
    wait(flip_in.at[pl.ds(0, R - 1)], fl_s)

    @pl.when(jnp.logical_not(to_self))
    def _():
        wait(route_src, rt_s)

    wait(half_v.at[pl.ds(0, Z - 1)], rs_s)
    wait(half_v.at[pl.ds(0, Z - 1)], x_s)
    wait(prod_in.at[pl.ds(0, R - 1)], g_s.at[0])
    if W > 1:
        wait(quad_in.at[pl.ds(0, W - 1)], g_s.at[1])
    wait(cross_in.at[pl.ds(0, 3)], g_s.at[2])
    wait(pfull_v.at[pl.ds(0, R - 1)], g_s.at[4])
    wait(half_v, xp_s)
    wait(half_v, xp_r)


def write_out(x_v, g_v, x_hbm, g_hbm, sem):
    g_copy = pltpu.make_async_copy(g_v, g_hbm, sem.at[0])
    g_copy.start()
    x_copy = pltpu.make_async_copy(x_v, x_hbm, sem.at[1])
    x_copy.start()
    g_copy.wait()
    x_copy.wait()


def solution(mesh):
    R, C = mesh.shape["row"], mesh.shape["col"]
    Z = C // 2
    W = Z // 4
    SL = 8 * BLK // C
    NS = BLK // SL
    HALF = 4 * NS
    GL = BLK // R

    def per_device(trail_adjoint, panel, panel_adjoint, diag_block):
        any_spec = pl.BlockSpec(memory_space=pl.ANY)
        hbm = pl.BlockSpec(memory_space=pltpu.MemorySpace.HBM)
        vmem = pl.BlockSpec(memory_space=pltpu.MemorySpace.VMEM)
        vm = lambda *shape: pltpu.VMEM(shape, F32)
        dma = pltpu.SemaphoreType.DMA
        in_hbm = lambda x: pltpu.with_memory_space_constraint(x, pltpu.MemorySpace.HBM)
        x, gram = pl.pallas_call(
            functools.partial(kernel, R, C),
            out_shape=(
                jax.ShapeDtypeStruct((2 * HALF, SL, BLK), F32),
                jax.ShapeDtypeStruct((BLK, BLK), F32),
            ),
            in_specs=[hbm] * 4,
            out_specs=(vmem, vmem),
            scratch_shapes=[
                vm(8, 4 * BLK, BLK),
                pltpu.VMEM((8 * BLK, 4 * BLK), BF16),
                pltpu.VMEM((8 * BLK, 4 * BLK), BF16),
                vm(2 * HALF, SL, BLK),
                vm(SL, BLK),
                vm(BLK, BLK),
                pltpu.VMEM((2 * BLK, 8 * BLK), BF16),
                vm(BLK, BLK),
                vm(R, SL, BLK),
                vm(R, SL, BLK),
                vm(R, SL, BLK),
                vm(SL, BLK),
                vm(SL, BLK),
                vm(HALF, SL, BLK),
                vm(HALF, SL, BLK),
                vm(HALF, SL, BLK),
                vm(W, SL, BLK),
                vm(max(W - 1, 1), SL, BLK),
                vm(2, SL, BLK),
                vm(2 * W, SL, BLK),
                vm(R, GL, BLK),
                vm(R, GL, BLK),
                vm(GL, BLK),
                vm(W, GL, BLK),
                vm(GL, BLK),
                vm(4, GL, BLK),
                vm(GL, BLK),
                vm(GL, BLK),
                vm(R, GL, BLK),
                dma((12,)),
                dma(()),
                dma(()),
                dma(()),
                dma(()),
                dma(()),
                dma(()),
                dma(()),
                dma(()),
                dma(()),
                dma(()),
                dma(()),
                dma((3,)),
                dma(()),
                dma((4 * W,)),
                dma(()),
                dma(()),
                dma((5,)),
                dma((5,)),
            ],
            compiler_params=pltpu.CompilerParams(
                collective_id=0, has_side_effects=True, vmem_limit_bytes=32 * 1024 * 1024
            ),
        )(
            in_hbm(trail_adjoint.reshape(8, 4 * BLK, BLK)),
            in_hbm(panel.reshape(2 * HALF, SL, BLK)),
            in_hbm(panel_adjoint.reshape(2 * HALF, SL, BLK)),
            in_hbm(diag_block),
        )
        x, gram = pl.pallas_call(
            write_out,
            out_shape=(
                jax.ShapeDtypeStruct((2 * HALF, SL, BLK), F32),
                jax.ShapeDtypeStruct((BLK, BLK), F32),
            ),
            in_specs=[any_spec] * 2,
            out_specs=(hbm, hbm),
            scratch_shapes=[dma((2,))],
            compiler_params=pltpu.CompilerParams(vmem_limit_bytes=8 * 1024 * 1024),
        )(x, gram)
        return x.reshape(8, BLK, BLK), gram

    return jax.shard_map(
        per_device,
        mesh=mesh,
        in_specs=(P(None, "row", None, "col"), P(None, "row", None), P(None, "row", None), P()),
        out_specs=(P(None, "row", None), P()),
        check_vma=False,
    )
```

```python
import functools
import math

import jax
import jax.numpy as jnp
from jax import lax
from jax.experimental import pallas as pl
from jax.experimental.pallas import tpu as pltpu
from jax.sharding import PartitionSpec as P

MESH = pl.DeviceIdType.MESH
F32 = jnp.float32
BF16 = jnp.bfloat16
HI = lax.Precision.HIGHEST
BLK = 128
RS_PAUSE = 400
AG_PAUSE = 600


def dot(a, b):
    return jnp.dot(a, b, precision=HI, preferred_element_type=F32)


def dot_t(a, b):
    return lax.dot_general(
        a, b, (((0,), (0,)), ((), ())), precision=HI, preferred_element_type=F32
    )


def invert_lower(d):
    n = d.shape[0]
    row = lax.broadcasted_iota(jnp.int32, (n, n), 0)
    col = lax.broadcasted_iota(jnp.int32, (n, n), 1)
    eye = row == col
    zero = jnp.zeros_like(d)
    diag = jnp.where(eye, d, zero)
    recip_row = 1.0 / jnp.sum(diag, axis=1, keepdims=True)
    recip_col = 1.0 / jnp.sum(diag, axis=0, keepdims=True)

    def below(shift):
        same = lax.shift_right_logical(row, shift + 1) == lax.shift_right_logical(col, shift + 1)
        other = lax.shift_right_logical(row, shift) != lax.shift_right_logical(col, shift)
        return jnp.where(same & other & (row > col), d, zero)

    inv = jnp.where(eye, jnp.broadcast_to(recip_row, (n, n)), -(below(0) * recip_row) * recip_col)
    shift = 1
    while (1 << shift) < n:
        inv = inv - dot(inv, dot(below(shift), inv))
        shift += 1
    return inv


def split(x):
    hi = x.astype(BF16)
    return hi, (x - hi.astype(F32)).astype(BF16)


def bdot(a, b):
    return jnp.dot(a, b, preferred_element_type=F32)


def kernel(
    rows,
    cols,
    s_hbm,
    panel_hbm,
    given_hbm,
    diag_hbm,
    x_v,
    g_out,
    s_v,
    s_hi,
    s_lo,
    p_v,
    b_v,
    d_v,
    pt_v,
    inv_v,
    lc,
    flip_v,
    flip_in,
    route_src,
    route_in,
    half_v,
    give_v,
    pair_in,
    agg_far,
    agg_near,
    agg_out,
    fin_in,
    prod_v,
    prod_in,
    quad_v,
    quad_in,
    cross_v,
    cross_in,
    ppair_v,
    ppair_in,
    pfull_v,
    loc,
    sc_s,
    sc_r,
    ag_s,
    ag_r,
    fl_s,
    fl_r,
    rt_s,
    rt_r,
    pr_s,
    pr_r,
    rs_s,
    rs_r,
    x_s,
    x_r,
    xp_s,
    xp_r,
    g_s,
    g_r,
):
    R, C = rows, cols
    Z = C // 2
    W = Z // 4
    SL = 8 * BLK // C
    NS = BLK // SL
    HALF = 4 * NS
    HR = 4 * BLK
    side = math.isqrt(R)
    r = lax.axis_index("row")
    c = lax.axis_index("col")
    z = c // 2
    k = c % 2

    def dev(row, chip, core):
        return (row, chip * 2 + core)

    hops = lambda d: min(d, side - d)
    steps = [(dx, dy) for dx in range(side) for dy in range(side) if dx + dy > 0]
    steps.sort(key=lambda d: -(hops(d[0]) + hops(d[1])))

    def at(step):
        dx, dy = step
        return ((r // side + dx) & (side - 1)) * side + ((r + dy) & (side - 1))

    sign = 1 - 2 * k

    def away(delta):
        return (z + sign * delta) & (Z - 1)

    def chip(delta):
        return dev(r, away(delta), k)

    def copy(src, dst, send, recv, device):
        return pltpu.make_async_remote_copy(
            src_ref=src,
            dst_ref=dst,
            send_sem=send,
            recv_sem=recv,
            device_id=device,
            device_id_type=MESH,
        )

    def wait(ref, sem):
        pltpu.make_async_copy(ref, ref, sem).wait()

    def offset_of(row, at):
        return (at - row // 2 + R // 4) & (Z - 1)

    def slice_in_half(o):
        m = o & (R // 2 - 1)
        return (2 * (m // NS) + o // (R // 2)) * NS + (m & (NS - 1))

    def slice_for(delta):
        return slice_in_half(offset_of(r, away(delta)))

    barrier = pltpu.get_barrier_semaphore()
    other = dev(r, z, 1 - k)
    for step in steps:
        pl.semaphore_signal(barrier, inc=1, device_id=(at(step), c), device_id_type=MESH)
    for i in range(W, 0, -1):
        for delta in (i, -i):
            for core in (0, 1):
                near_by = dev(r, (z + delta) & (Z - 1), core)
                pl.semaphore_signal(barrier, inc=1, device_id=near_by, device_id_type=MESH)
    pl.semaphore_signal(barrier, inc=1, device_id=other, device_id_type=MESH)

    cp_s = [pltpu.make_async_copy(s_hbm.at[a], s_v.at[a], loc.at[1 + a]) for a in range(8)]
    cp_panel = pltpu.make_async_copy(panel_hbm, p_v, loc.at[0])
    for one in cp_s:
        one.start()
    cp_panel.start()
    my_slice = slice_for(0)
    sid = k * HALF + my_slice
    cp_b = pltpu.make_async_copy(given_hbm.at[sid], b_v, loc.at[9])
    cp_b.start()
    cp_d = pltpu.make_async_copy(diag_hbm, d_v, loc.at[10])
    cp_d.start()

    greeted = R - 1 + 4 * W + 1
    owner = c & (R - 1)
    which = c // R
    own = owner == r

    def piece(s):
        return panel_hbm.at[(2 * (s // NS) + which) * NS + (s & (NS - 1))]

    @pl.when(own)
    def _():
        pl.semaphore_wait(barrier, greeted)
        for step in steps:
            s = at(step)
            copy(piece(s), lc.at[s], sc_s, sc_r, (s, c)).start()
        mine = pltpu.make_async_copy(piece(r), lc.at[r], loc.at[11])
        mine.start()
        mine.wait()

    for a in range(8):
        cp_s[a].wait()

        for b in range(4):
            hi, lo = split(s_v[a, pl.ds(b, BLK, stride=4), :])
            s_hi[pl.ds(a * BLK, BLK), pl.ds(b * BLK, BLK)] = hi
            s_lo[pl.ds(a * BLK, BLK), pl.ds(b * BLK, BLK)] = lo
    cp_panel.wait()
    for a in range(8):
        hi, lo = split(p_v[pl.ds(a * NS, NS)].reshape(BLK, BLK).T)
        pt_v[pl.ds(0, BLK), pl.ds(a * BLK, BLK)] = hi
        pt_v[pl.ds(BLK, BLK), pl.ds(a * BLK, BLK)] = lo
    for b in range(2):
        wide = pl.ds(b * 2 * BLK, 2 * BLK)
        both = bdot(pt_v[...], s_hi[:, wide])
        part = both[:BLK] + (both[BLK:] + bdot(pt_v[pl.ds(0, BLK), :], s_lo[:, wide]))
        flip_v[pl.ds(b * 2 * NS, 2 * NS)] = part.T.reshape(2 * NS, SL, BLK)

    @pl.when(jnp.logical_not(own))
    def _():
        pl.semaphore_wait(barrier, greeted)

    for step in steps:
        copy(flip_v.at[at(step)], flip_in.at[r], fl_s, fl_r, (at(step), c)).start()

    @pl.when(jnp.logical_not(own))
    def _():
        wait(lc.at[r], sc_r)

    for step in steps:
        copy(lc.at[r], lc.at[r], ag_s, ag_r, (at(step), c)).start()

    cp_d.wait()
    inv_v[...] = invert_lower(d_v[...])

    wait(flip_in.at[pl.ds(0, R - 1)], fl_r)
    flip_in[r] = flip_v[r]
    total_flip = flip_in[0]
    for i in range(1, R):
        total_flip = total_flip + flip_in[i]
    route_src[...] = total_flip

    cross_part = dot_t(total_flip, lc[r])
    cp_b.wait()
    prod = dot_t(b_v[...], p_v[sid]) - (cross_part + cross_part.T)
    prod_v[...] = prod.reshape(R, BLK // R, BLK)
    for step in steps:
        copy(prod_v.at[at(step)], prod_in.at[r], g_s.at[0], g_r.at[0], (at(step), c)).start()

    wait(lc.at[pl.ds(0, R - 1)], ag_r)

    to_r = owner
    to_z = (z - R // 4 + (r & (R // 2 - 1))) & (Z - 1)
    to_k = r // (R // 2)
    to_self = (to_r == r) & (to_z == z) & (to_k == k)

    @pl.when(jnp.logical_not(to_self))
    def _():
        copy(route_src, route_in, rt_s, rt_r, dev(to_r, to_z, to_k)).start()

    @pl.when(to_self)
    def _():
        route_in[...] = route_src[...]

    w_hi, w_lo = split(lc[...].reshape(HR, BLK))
    w_both = jnp.concatenate([w_hi, w_lo], axis=1)

    def direct_half(base):
        at = pl.ds(pl.multiple_of(base * HR, HR), HR)
        both = bdot(s_hi[at, :], w_both)
        out = both[:, :BLK] + (both[:, BLK:] + bdot(s_lo[at, :], w_hi))
        return out.reshape(HALF, SL, BLK)

    give_v[...] = direct_half(1 - k)
    pair = copy(give_v, pair_in, pr_s, pr_r, other)
    pair.start()
    kept = direct_half(k)
    pair.wait()
    half_v[...] = kept + pair_in[...]

    for d in range(2 * W, W, -1):
        copy(half_v.at[slice_for(d)], agg_far.at[d - W - 1], rs_s, rs_r.at[0], chip(d - W)).start()
        if d < 2 * W:
            copy(
                half_v.at[slice_for(-d)], agg_near.at[d - W - 1], rs_s, rs_r.at[1], chip(W - d)
            ).start()

    pl.delay(RS_PAUSE)
    for d in range(W - 1, 0, -1):
        copy(half_v.at[slice_for(d)], fin_in.at[d - 1], rs_s, rs_r.at[2], chip(d)).start()
        copy(half_v.at[slice_for(-d)], fin_in.at[W + d - 2], rs_s, rs_r.at[2], chip(-d)).start()

    wait(prod_in.at[pl.ds(0, R - 1)], g_r.at[0])
    prod_in[r] = prod_v[r]
    acc = prod_in[0]
    for i in range(1, R):
        acc = acc + prod_in[i]
    group, lane = z // W, z & (W - 1)
    quad_v[...] = acc
    for i in range(1, W):
        mate = dev(r, group * W + ((lane + i) & (W - 1)), k)
        copy(quad_v, quad_in.at[lane], g_s.at[1], g_r.at[1], mate).start()

    wait(agg_far, rs_r.at[0])
    far = half_v[slice_for(W)]
    for i in range(W):
        far = far + agg_far[i]
    agg_out[0] = far
    copy(agg_out.at[0], fin_in.at[2 * W - 2], rs_s, rs_r.at[2], chip(W)).start()
    near = half_v[slice_for(-W)]
    if W > 1:
        wait(agg_near.at[pl.ds(0, W - 1)], rs_r.at[1])
        for i in range(W - 1):
            near = near + agg_near[i]
    agg_out[1] = near
    copy(agg_out.at[1], fin_in.at[2 * W - 1], rs_s, rs_r.at[2], chip(-W)).start()

    if W > 1:
        wait(quad_in.at[pl.ds(0, W - 1)], g_r.at[1])
    quad_in[lane] = quad_v[...]
    acc = quad_in[0]
    for i in range(1, W):
        acc = acc + quad_in[i]
    cross_v[...] = acc
    for i in range(1, 4):
        copy(cross_v, cross_in.at[group], g_s.at[2], g_r.at[2], chip(i * W)).start()

    @pl.when(jnp.logical_not(to_self))
    def _():
        wait(route_in, rt_r)

    wait(fin_in, rs_r.at[2])
    total = half_v[my_slice]
    for i in range(2 * W):
        total = total + fin_in[i]
    total = b_v[...] - (total + route_in[...])
    x_v[sid] = dot(total, inv_v[...])

    def sid_at(delta):
        return k * HALF + slice_for(delta)

    def send_x(s, sem, device):
        copy(x_v.at[s], x_v.at[s], x_s, x_r.at[sem], device).start()

    def forward(s):
        copy(x_v.at[s], x_v.at[s], xp_s, xp_r, other).start()

    send_x(sid, W, chip(W))
    send_x(sid, 3 * W, chip(-W))
    forward(sid)
    pl.delay(AG_PAUSE)
    for d in range(W - 1, 0, -1):
        send_x(sid, d, chip(d))
        send_x(sid, 2 * W + d, chip(-d))

    wait(cross_in.at[pl.ds(0, 3)], g_r.at[2])
    cross_in[group] = cross_v[...]
    ppair_v[...] = (cross_in[0] + cross_in[1]) + (cross_in[2] + cross_in[3])
    hand = copy(ppair_v, ppair_in, g_s.at[3], g_r.at[3], other)
    hand.start()

    far_sid = sid_at(-W)
    wait(x_v.at[far_sid], x_r.at[W])
    for d in range(W, 0, -1):
        send_x(far_sid, W + d, chip(d))
    near_sid = sid_at(W)
    wait(x_v.at[near_sid], x_r.at[3 * W])
    for d in range(W - 1, 0, -1):
        send_x(near_sid, 3 * W + d, chip(-d))
    hand.wait()
    pfull_v[r] = ppair_v[...] + ppair_in[...]
    for step in steps:
        copy(pfull_v.at[r], pfull_v.at[r], g_s.at[4], g_r.at[4], (at(step), c)).start()

    forward(far_sid)
    forward(near_sid)
    for d in range(1, W):
        wait(x_v.at[sid_at(-d)], x_r.at[d])
        forward(sid_at(-d))
        wait(x_v.at[sid_at(d)], x_r.at[2 * W + d])
        forward(sid_at(d))

    for d in range(1, W):
        wait(x_v.at[sid_at(-W - d)], x_r.at[W + d])
        forward(sid_at(-W - d))
        wait(x_v.at[sid_at(W + d)], x_r.at[3 * W + d])
        forward(sid_at(W + d))
    wait(x_v.at[sid_at(-2 * W)], x_r.at[2 * W])
    forward(sid_at(-2 * W))

    wait(pfull_v.at[pl.ds(0, R - 1)], g_r.at[4])
    gram = -dot_t(inv_v[...], pfull_v[...].reshape(BLK, BLK))
    row = lax.broadcasted_iota(jnp.int32, (BLK, BLK), 0)
    col = lax.broadcasted_iota(jnp.int32, (BLK, BLK), 1)
    g_out[...] = jnp.where(row >= col, gram, jnp.zeros_like(gram))

    @pl.when(own)
    def _():
        wait(lc.at[pl.ds(0, R - 1)], sc_s)

    wait(lc.at[pl.ds(0, R - 1)], ag_s)
    wait(flip_in.at[pl.ds(0, R - 1)], fl_s)

    @pl.when(jnp.logical_not(to_self))
    def _():
        wait(route_src, rt_s)

    wait(half_v.at[pl.ds(0, Z - 1)], rs_s)
    wait(half_v.at[pl.ds(0, Z - 1)], x_s)
    wait(prod_in.at[pl.ds(0, R - 1)], g_s.at[0])
    if W > 1:
        wait(quad_in.at[pl.ds(0, W - 1)], g_s.at[1])
    wait(cross_in.at[pl.ds(0, 3)], g_s.at[2])
    wait(pfull_v.at[pl.ds(0, R - 1)], g_s.at[4])
    wait(half_v, xp_s)
    wait(half_v, xp_r)


def write_out(x_v, g_v, x_hbm, g_hbm, sem):
    g_copy = pltpu.make_async_copy(g_v, g_hbm, sem.at[0])
    g_copy.start()
    x_copy = pltpu.make_async_copy(x_v, x_hbm, sem.at[1])
    x_copy.start()
    g_copy.wait()
    x_copy.wait()


def solution(mesh):
    R, C = mesh.shape["row"], mesh.shape["col"]
    Z = C // 2
    W = Z // 4
    SL = 8 * BLK // C
    NS = BLK // SL
    HALF = 4 * NS
    GL = BLK // R

    def per_device(trail_adjoint, panel, panel_adjoint, diag_block):
        any_spec = pl.BlockSpec(memory_space=pl.ANY)
        hbm = pl.BlockSpec(memory_space=pltpu.MemorySpace.HBM)
        vmem = pl.BlockSpec(memory_space=pltpu.MemorySpace.VMEM)
        vm = lambda *shape: pltpu.VMEM(shape, F32)
        dma = pltpu.SemaphoreType.DMA
        in_hbm = lambda x: pltpu.with_memory_space_constraint(x, pltpu.MemorySpace.HBM)
        x, gram = pl.pallas_call(
            functools.partial(kernel, R, C),
            out_shape=(
                jax.ShapeDtypeStruct((2 * HALF, SL, BLK), F32),
                jax.ShapeDtypeStruct((BLK, BLK), F32),
            ),
            in_specs=[hbm] * 4,
            out_specs=(vmem, vmem),
            scratch_shapes=[
                vm(8, 4 * BLK, BLK),
                pltpu.VMEM((8 * BLK, 4 * BLK), BF16),
                pltpu.VMEM((8 * BLK, 4 * BLK), BF16),
                vm(2 * HALF, SL, BLK),
                vm(SL, BLK),
                vm(BLK, BLK),
                pltpu.VMEM((2 * BLK, 8 * BLK), BF16),
                vm(BLK, BLK),
                vm(R, SL, BLK),
                vm(R, SL, BLK),
                vm(R, SL, BLK),
                vm(SL, BLK),
                vm(SL, BLK),
                vm(HALF, SL, BLK),
                vm(HALF, SL, BLK),
                vm(HALF, SL, BLK),
                vm(W, SL, BLK),
                vm(max(W - 1, 1), SL, BLK),
                vm(2, SL, BLK),
                vm(2 * W, SL, BLK),
                vm(R, GL, BLK),
                vm(R, GL, BLK),
                vm(GL, BLK),
                vm(W, GL, BLK),
                vm(GL, BLK),
                vm(4, GL, BLK),
                vm(GL, BLK),
                vm(GL, BLK),
                vm(R, GL, BLK),
                dma((12,)),
                dma(()),
                dma(()),
                dma(()),
                dma(()),
                dma(()),
                dma(()),
                dma(()),
                dma(()),
                dma(()),
                dma(()),
                dma(()),
                dma((3,)),
                dma(()),
                dma((4 * W,)),
                dma(()),
                dma(()),
                dma((5,)),
                dma((5,)),
            ],
            compiler_params=pltpu.CompilerParams(
                collective_id=0, has_side_effects=True, vmem_limit_bytes=32 * 1024 * 1024
            ),
        )(
            in_hbm(trail_adjoint.reshape(8, 4 * BLK, BLK)),
            in_hbm(panel.reshape(2 * HALF, SL, BLK)),
            in_hbm(panel_adjoint.reshape(2 * HALF, SL, BLK)),
            in_hbm(diag_block),
        )
        x, gram = pl.pallas_call(
            write_out,
            out_shape=(
                jax.ShapeDtypeStruct((2 * HALF, SL, BLK), F32),
                jax.ShapeDtypeStruct((BLK, BLK), F32),
            ),
            in_specs=[any_spec] * 2,
            out_specs=(hbm, hbm),
            scratch_shapes=[dma((2,))],
            compiler_params=pltpu.CompilerParams(vmem_limit_bytes=8 * 1024 * 1024),
        )(x, gram)
        return x.reshape(8, BLK, BLK), gram

    return jax.shard_map(
        per_device,
        mesh=mesh,
        in_specs=(P(None, "row", None, "col"), P(None, "row", None), P(None, "row", None), P()),
        out_specs=(P(None, "row", None), P()),
        check_vma=False,
    )
```

```python
import functools
import math

import jax
import jax.numpy as jnp
from jax import lax
from jax.experimental import pallas as pl
from jax.experimental.pallas import tpu as pltpu
from jax.sharding import PartitionSpec as P

MESH = pl.DeviceIdType.MESH
F32 = jnp.float32
BF16 = jnp.bfloat16
HI = lax.Precision.HIGHEST
BLK = 128
FIRST = 1
RS_PAUSE = 400
AG_PAUSE = 600


def dot(a, b):
    return jnp.dot(a, b, precision=HI, preferred_element_type=F32)


def dot_t(a, b):
    return lax.dot_general(
        a, b, (((0,), (0,)), ((), ())), precision=HI, preferred_element_type=F32
    )


def invert_lower(d):
    n = d.shape[0]
    row = lax.broadcasted_iota(jnp.int32, (n, n), 0)
    col = lax.broadcasted_iota(jnp.int32, (n, n), 1)
    eye = row == col
    zero = jnp.zeros_like(d)
    diag = jnp.where(eye, d, zero)
    recip_row = 1.0 / jnp.sum(diag, axis=1, keepdims=True)
    recip_col = 1.0 / jnp.sum(diag, axis=0, keepdims=True)

    def below(shift):
        same = lax.shift_right_logical(row, shift + 1) == lax.shift_right_logical(col, shift + 1)
        other = lax.shift_right_logical(row, shift) != lax.shift_right_logical(col, shift)
        return jnp.where(same & other & (row > col), d, zero)

    inv = jnp.where(eye, jnp.broadcast_to(recip_row, (n, n)), -(below(0) * recip_row) * recip_col)
    shift = 1
    while (1 << shift) < n:
        inv = inv - dot(inv, dot(below(shift), inv))
        shift += 1
    return inv


def split(x):
    hi = x.astype(BF16)
    return hi, (x - hi.astype(F32)).astype(BF16)


def bdot(a, b):
    return jnp.dot(a, b, preferred_element_type=F32)


def kernel(
    rows,
    cols,
    s_hbm,
    panel_hbm,
    given_hbm,
    diag_hbm,
    x_v,
    g_out,
    s_v,
    s_hi,
    s_lo,
    p_v,
    b_v,
    d_v,
    pt_v,
    inv_v,
    lc,
    flip_v,
    flip_in,
    route_src,
    route_in,
    half_v,
    give_v,
    pair_in,
    agg_far,
    agg_near,
    agg_out,
    fin_in,
    prod_v,
    prod_in,
    quad_v,
    quad_in,
    cross_v,
    cross_in,
    ppair_v,
    ppair_in,
    pfull_v,
    loc,
    sc_s,
    sc_r,
    ag_s,
    ag_r,
    fl_s,
    fl_r,
    rt_s,
    rt_r,
    pr_s,
    pr_r,
    rs_s,
    rs_r,
    x_s,
    x_d,
    x_r,
    xp_s,
    xp_r,
    g_s,
    g_r,
):
    R, C = rows, cols
    Z = C // 2
    W = Z // 4
    SL = 8 * BLK // C
    NS = BLK // SL
    HALF = 4 * NS
    HR = 4 * BLK
    side = math.isqrt(R)
    r = lax.axis_index("row")
    c = lax.axis_index("col")
    z = c // 2
    k = c % 2

    def dev(row, chip, core):
        return (row, chip * 2 + core)

    hops = lambda d: min(d, side - d)
    steps = [(dx, dy) for dx in range(side) for dy in range(side) if dx + dy > 0]
    steps.sort(key=lambda d: -(hops(d[0]) + hops(d[1])))

    def at(step):
        dx, dy = step
        return ((r // side + dx) & (side - 1)) * side + ((r + dy) & (side - 1))

    sign = 1 - 2 * k

    def away(delta):
        return (z + sign * delta) & (Z - 1)

    def chip(delta):
        return dev(r, away(delta), k)

    def copy(src, dst, send, recv, device):
        return pltpu.make_async_remote_copy(
            src_ref=src,
            dst_ref=dst,
            send_sem=send,
            recv_sem=recv,
            device_id=device,
            device_id_type=MESH,
        )

    def wait(ref, sem):
        pltpu.make_async_copy(ref, ref, sem).wait()

    def offset_of(row, at):
        return (at - row // 2 + R // 4) & (Z - 1)

    def slice_in_half(o):
        m = o & (R // 2 - 1)
        return (2 * (m // NS) + o // (R // 2)) * NS + (m & (NS - 1))

    def slice_for(delta):
        return slice_in_half(offset_of(r, away(delta)))

    barrier = pltpu.get_barrier_semaphore()
    other = dev(r, z, 1 - k)
    for step in steps:
        pl.semaphore_signal(barrier, inc=1, device_id=(at(step), c), device_id_type=MESH)
    for i in range(W, 0, -1):
        for delta in (i, -i):
            for core in (0, 1):
                near_by = dev(r, (z + delta) & (Z - 1), core)
                pl.semaphore_signal(barrier, inc=1, device_id=near_by, device_id_type=MESH)
    pl.semaphore_signal(barrier, inc=1, device_id=other, device_id_type=MESH)

    cp_s = [pltpu.make_async_copy(s_hbm.at[a], s_v.at[a], loc.at[1 + a]) for a in range(8)]
    cp_panel = pltpu.make_async_copy(panel_hbm, p_v, loc.at[0])
    for one in cp_s:
        one.start()
    cp_panel.start()
    my_slice = slice_for(0)
    sid = k * HALF + my_slice
    cp_b = pltpu.make_async_copy(given_hbm.at[sid], b_v, loc.at[9])
    cp_b.start()
    cp_d = pltpu.make_async_copy(diag_hbm, d_v, loc.at[10])
    cp_d.start()

    greeted = R - 1 + 4 * W + 1
    owner = c & (R - 1)
    which = c // R
    own = owner == r

    def piece(s):
        return panel_hbm.at[(2 * (s // NS) + which) * NS + (s & (NS - 1))]

    @pl.when(own)
    def _():
        pl.semaphore_wait(barrier, greeted)
        for step in steps:
            s = at(step)
            copy(piece(s), lc.at[s], sc_s, sc_r, (s, c)).start()
        mine = pltpu.make_async_copy(piece(r), lc.at[r], loc.at[11])
        mine.start()
        mine.wait()

    for a in range(8):
        cp_s[a].wait()

        for b in range(4):
            hi, lo = split(s_v[a, pl.ds(b, BLK, stride=4), :])
            s_hi[pl.ds(a * BLK, BLK), pl.ds(b * BLK, BLK)] = hi
            s_lo[pl.ds(a * BLK, BLK), pl.ds(b * BLK, BLK)] = lo
    cp_panel.wait()
    for a in range(8):
        hi, lo = split(p_v[pl.ds(a * NS, NS)].reshape(BLK, BLK).T)
        pt_v[pl.ds(0, BLK), pl.ds(a * BLK, BLK)] = hi
        pt_v[pl.ds(BLK, BLK), pl.ds(a * BLK, BLK)] = lo
    for b in range(2):
        wide = pl.ds(b * 2 * BLK, 2 * BLK)
        both = bdot(pt_v[...], s_hi[:, wide])
        part = both[:BLK] + (both[BLK:] + bdot(pt_v[pl.ds(0, BLK), :], s_lo[:, wide]))
        flip_v[pl.ds(b * 2 * NS, 2 * NS)] = part.T.reshape(2 * NS, SL, BLK)

    @pl.when(jnp.logical_not(own))
    def _():
        pl.semaphore_wait(barrier, greeted)

    for step in steps:
        copy(flip_v.at[at(step)], flip_in.at[r], fl_s, fl_r, (at(step), c)).start()

    @pl.when(jnp.logical_not(own))
    def _():
        wait(lc.at[r], sc_r)

    for step in steps:
        copy(lc.at[r], lc.at[r], ag_s, ag_r, (at(step), c)).start()

    cp_d.wait()
    inv_v[...] = invert_lower(d_v[...])

    wait(flip_in.at[pl.ds(0, R - 1)], fl_r)
    flip_in[r] = flip_v[r]
    total_flip = flip_in[0]
    for i in range(1, R):
        total_flip = total_flip + flip_in[i]
    route_src[...] = total_flip

    cross_part = dot_t(total_flip, lc[r])
    cp_b.wait()
    prod = dot_t(b_v[...], p_v[sid]) - (cross_part + cross_part.T)
    prod_v[...] = prod.reshape(R, BLK // R, BLK)
    for step in steps:
        copy(prod_v.at[at(step)], prod_in.at[r], g_s.at[0], g_r.at[0], (at(step), c)).start()

    wait(lc.at[pl.ds(0, R - 1)], ag_r)

    to_r = owner
    to_z = (z - R // 4 + (r & (R // 2 - 1))) & (Z - 1)
    to_k = r // (R // 2)
    to_self = (to_r == r) & (to_z == z) & (to_k == k)

    @pl.when(jnp.logical_not(to_self))
    def _():
        copy(route_src, route_in, rt_s, rt_r, dev(to_r, to_z, to_k)).start()

    @pl.when(to_self)
    def _():
        route_in[...] = route_src[...]

    w_hi, w_lo = split(lc[...].reshape(HR, BLK))
    w_both = jnp.concatenate([w_hi, w_lo], axis=1)

    def direct_half(base):
        at = pl.ds(pl.multiple_of(base * HR, HR), HR)
        both = bdot(s_hi[at, :], w_both)
        out = both[:, :BLK] + (both[:, BLK:] + bdot(s_lo[at, :], w_hi))
        return out.reshape(HALF, SL, BLK)

    give_v[...] = direct_half(1 - k)
    pair = copy(give_v, pair_in, pr_s, pr_r, other)
    pair.start()
    kept = direct_half(k)
    pair.wait()
    half_v[...] = kept + pair_in[...]

    for d in range(2 * W, W, -1):
        copy(half_v.at[slice_for(d)], agg_far.at[d - W - 1], rs_s, rs_r.at[0], chip(d - W)).start()
        if d < 2 * W:
            copy(
                half_v.at[slice_for(-d)], agg_near.at[d - W - 1], rs_s, rs_r.at[1], chip(W - d)
            ).start()

    pl.delay(RS_PAUSE)
    for d in range(W - 1, 0, -1):
        copy(half_v.at[slice_for(d)], fin_in.at[d - 1], rs_s, rs_r.at[2], chip(d)).start()
        copy(half_v.at[slice_for(-d)], fin_in.at[W + d - 2], rs_s, rs_r.at[2], chip(-d)).start()

    wait(prod_in.at[pl.ds(0, R - 1)], g_r.at[0])
    prod_in[r] = prod_v[r]
    acc = prod_in[0]
    for i in range(1, R):
        acc = acc + prod_in[i]
    group, lane = z // W, z & (W - 1)
    quad_v[...] = acc
    for i in range(1, W):
        mate = dev(r, group * W + ((lane + i) & (W - 1)), k)
        copy(quad_v, quad_in.at[lane], g_s.at[1], g_r.at[1], mate).start()

    wait(agg_far, rs_r.at[0])
    far = half_v[slice_for(W)]
    for i in range(W):
        far = far + agg_far[i]
    agg_out[0] = far
    copy(agg_out.at[0], fin_in.at[2 * W - 2], rs_s, rs_r.at[2], chip(W)).start()
    near = half_v[slice_for(-W)]
    if W > 1:
        wait(agg_near.at[pl.ds(0, W - 1)], rs_r.at[1])
        for i in range(W - 1):
            near = near + agg_near[i]
    agg_out[1] = near
    copy(agg_out.at[1], fin_in.at[2 * W - 1], rs_s, rs_r.at[2], chip(-W)).start()

    if W > 1:
        wait(quad_in.at[pl.ds(0, W - 1)], g_r.at[1])
    quad_in[lane] = quad_v[...]
    acc = quad_in[0]
    for i in range(1, W):
        acc = acc + quad_in[i]
    cross_v[...] = acc
    for i in range(1, 4):
        copy(cross_v, cross_in.at[group], g_s.at[2], g_r.at[2], chip(i * W)).start()

    @pl.when(jnp.logical_not(to_self))
    def _():
        wait(route_in, rt_r)

    wait(fin_in, rs_r.at[2])
    total = half_v[my_slice]
    for i in range(2 * W):
        total = total + fin_in[i]
    total = b_v[...] - (total + route_in[...])
    x_v[sid] = dot(total, inv_v[...])

    def sid_at(delta):
        return k * HALF + slice_for(delta)

    def send_x(s, sem, device):
        copy(x_v.at[s], x_v.at[s], x_s, x_r.at[sem], device).start()

    def forward(s):
        copy(x_v.at[s], x_v.at[s], xp_s, xp_r, other).start()

    chosen = []

    def send_if(cond, s, sem, device):
        one = copy(x_v.at[s], x_v.at[s], x_d.at[len(chosen)], x_r.at[sem], device)
        chosen.append((cond, one))

        @pl.when(cond)
        def _():
            one.start()

    send_x(sid, W, chip(W))
    send_x(sid, 3 * W, chip(-W))
    for d in range(2 * W, W, -1):
        send_if(away(d) < FIRST, sid, d, chip(d))
        if d < 2 * W:
            send_if(away(-d) < FIRST, sid, 2 * W + d, chip(-d))
    forward(sid)
    pl.delay(AG_PAUSE)
    for d in range(W - 1, 0, -1):
        send_x(sid, d, chip(d))
        send_x(sid, 2 * W + d, chip(-d))

    wait(cross_in.at[pl.ds(0, 3)], g_r.at[2])
    cross_in[group] = cross_v[...]
    ppair_v[...] = (cross_in[0] + cross_in[1]) + (cross_in[2] + cross_in[3])
    hand = copy(ppair_v, ppair_in, g_s.at[3], g_r.at[3], other)
    hand.start()

    far_sid = sid_at(-W)
    wait(x_v.at[far_sid], x_r.at[W])
    for d in range(W, 0, -1):
        send_if(away(d) >= FIRST, far_sid, W + d, chip(d))
    near_sid = sid_at(W)
    wait(x_v.at[near_sid], x_r.at[3 * W])
    for d in range(W - 1, 0, -1):
        send_if(away(-d) >= FIRST, near_sid, 3 * W + d, chip(-d))
    hand.wait()
    pfull_v[r] = ppair_v[...] + ppair_in[...]
    for step in steps:
        copy(pfull_v.at[r], pfull_v.at[r], g_s.at[4], g_r.at[4], (at(step), c)).start()

    forward(far_sid)
    forward(near_sid)
    for d in range(1, W):
        wait(x_v.at[sid_at(-d)], x_r.at[d])
        forward(sid_at(-d))
        wait(x_v.at[sid_at(d)], x_r.at[2 * W + d])
        forward(sid_at(d))

    for d in range(1, W):
        wait(x_v.at[sid_at(-W - d)], x_r.at[W + d])
        forward(sid_at(-W - d))
        wait(x_v.at[sid_at(W + d)], x_r.at[3 * W + d])
        forward(sid_at(W + d))
    wait(x_v.at[sid_at(-2 * W)], x_r.at[2 * W])
    forward(sid_at(-2 * W))

    wait(pfull_v.at[pl.ds(0, R - 1)], g_r.at[4])
    gram = -dot_t(inv_v[...], pfull_v[...].reshape(BLK, BLK))
    row = lax.broadcasted_iota(jnp.int32, (BLK, BLK), 0)
    col = lax.broadcasted_iota(jnp.int32, (BLK, BLK), 1)
    g_out[...] = jnp.where(row >= col, gram, jnp.zeros_like(gram))

    @pl.when(own)
    def _():
        wait(lc.at[pl.ds(0, R - 1)], sc_s)

    wait(lc.at[pl.ds(0, R - 1)], ag_s)
    wait(flip_in.at[pl.ds(0, R - 1)], fl_s)

    @pl.when(jnp.logical_not(to_self))
    def _():
        wait(route_src, rt_s)

    wait(half_v.at[pl.ds(0, Z - 1)], rs_s)
    wait(half_v.at[pl.ds(0, 2 * W)], x_s)
    for cond, one in chosen:
        pl.when(cond)(one.wait_send)
    wait(prod_in.at[pl.ds(0, R - 1)], g_s.at[0])
    if W > 1:
        wait(quad_in.at[pl.ds(0, W - 1)], g_s.at[1])
    wait(cross_in.at[pl.ds(0, 3)], g_s.at[2])
    wait(pfull_v.at[pl.ds(0, R - 1)], g_s.at[4])
    wait(half_v, xp_s)
    wait(half_v, xp_r)


def write_out(x_v, g_v, x_hbm, g_hbm, sem):
    g_copy = pltpu.make_async_copy(g_v, g_hbm, sem.at[0])
    g_copy.start()
    x_copy = pltpu.make_async_copy(x_v, x_hbm, sem.at[1])
    x_copy.start()
    g_copy.wait()
    x_copy.wait()


def solution(mesh):
    R, C = mesh.shape["row"], mesh.shape["col"]
    Z = C // 2
    W = Z // 4
    SL = 8 * BLK // C
    NS = BLK // SL
    HALF = 4 * NS
    GL = BLK // R

    def per_device(trail_adjoint, panel, panel_adjoint, diag_block):
        any_spec = pl.BlockSpec(memory_space=pl.ANY)
        hbm = pl.BlockSpec(memory_space=pltpu.MemorySpace.HBM)
        vmem = pl.BlockSpec(memory_space=pltpu.MemorySpace.VMEM)
        vm = lambda *shape: pltpu.VMEM(shape, F32)
        dma = pltpu.SemaphoreType.DMA
        in_hbm = lambda x: pltpu.with_memory_space_constraint(x, pltpu.MemorySpace.HBM)
        x, gram = pl.pallas_call(
            functools.partial(kernel, R, C),
            out_shape=(
                jax.ShapeDtypeStruct((2 * HALF, SL, BLK), F32),
                jax.ShapeDtypeStruct((BLK, BLK), F32),
            ),
            in_specs=[hbm] * 4,
            out_specs=(vmem, vmem),
            scratch_shapes=[
                vm(8, 4 * BLK, BLK),
                pltpu.VMEM((8 * BLK, 4 * BLK), BF16),
                pltpu.VMEM((8 * BLK, 4 * BLK), BF16),
                vm(2 * HALF, SL, BLK),
                vm(SL, BLK),
                vm(BLK, BLK),
                pltpu.VMEM((2 * BLK, 8 * BLK), BF16),
                vm(BLK, BLK),
                vm(R, SL, BLK),
                vm(R, SL, BLK),
                vm(R, SL, BLK),
                vm(SL, BLK),
                vm(SL, BLK),
                vm(HALF, SL, BLK),
                vm(HALF, SL, BLK),
                vm(HALF, SL, BLK),
                vm(W, SL, BLK),
                vm(max(W - 1, 1), SL, BLK),
                vm(2, SL, BLK),
                vm(2 * W, SL, BLK),
                vm(R, GL, BLK),
                vm(R, GL, BLK),
                vm(GL, BLK),
                vm(W, GL, BLK),
                vm(GL, BLK),
                vm(4, GL, BLK),
                vm(GL, BLK),
                vm(GL, BLK),
                vm(R, GL, BLK),
                dma((12,)),
                dma(()),
                dma(()),
                dma(()),
                dma(()),
                dma(()),
                dma(()),
                dma(()),
                dma(()),
                dma(()),
                dma(()),
                dma(()),
                dma((3,)),
                dma(()),
                dma((4 * W - 2,)),
                dma((4 * W,)),
                dma(()),
                dma(()),
                dma((5,)),
                dma((5,)),
            ],
            compiler_params=pltpu.CompilerParams(
                collective_id=0, has_side_effects=True, vmem_limit_bytes=32 * 1024 * 1024
            ),
        )(
            in_hbm(trail_adjoint.reshape(8, 4 * BLK, BLK)),
            in_hbm(panel.reshape(2 * HALF, SL, BLK)),
            in_hbm(panel_adjoint.reshape(2 * HALF, SL, BLK)),
            in_hbm(diag_block),
        )
        x, gram = pl.pallas_call(
            write_out,
            out_shape=(
                jax.ShapeDtypeStruct((2 * HALF, SL, BLK), F32),
                jax.ShapeDtypeStruct((BLK, BLK), F32),
            ),
            in_specs=[any_spec] * 2,
            out_specs=(hbm, hbm),
            scratch_shapes=[dma((2,))],
            compiler_params=pltpu.CompilerParams(vmem_limit_bytes=8 * 1024 * 1024),
        )(x, gram)
        return x.reshape(8, BLK, BLK), gram

    return jax.shard_map(
        per_device,
        mesh=mesh,
        in_specs=(P(None, "row", None, "col"), P(None, "row", None), P(None, "row", None), P()),
        out_specs=(P(None, "row", None), P()),
        check_vma=False,
    )
```

```python
import functools
import math

import jax
import jax.numpy as jnp
from jax import lax
from jax.experimental import pallas as pl
from jax.experimental.pallas import tpu as pltpu
from jax.sharding import PartitionSpec as P

MESH = pl.DeviceIdType.MESH
F32 = jnp.float32
BF16 = jnp.bfloat16
HI = lax.Precision.HIGHEST
BLK = 128
FIRST = 1
RS_PAUSE = 400
AG_PAUSE = 600


def dot(a, b):
    return jnp.dot(a, b, precision=HI, preferred_element_type=F32)


def dot_t(a, b):
    return lax.dot_general(
        a, b, (((0,), (0,)), ((), ())), precision=HI, preferred_element_type=F32
    )


def invert_lower(d):
    n = d.shape[0]
    row = lax.broadcasted_iota(jnp.int32, (n, n), 0)
    col = lax.broadcasted_iota(jnp.int32, (n, n), 1)
    eye = row == col
    zero = jnp.zeros_like(d)
    diag = jnp.where(eye, d, zero)
    recip_row = 1.0 / jnp.sum(diag, axis=1, keepdims=True)
    recip_col = 1.0 / jnp.sum(diag, axis=0, keepdims=True)

    def below(shift):
        same = lax.shift_right_logical(row, shift + 1) == lax.shift_right_logical(col, shift + 1)
        other = lax.shift_right_logical(row, shift) != lax.shift_right_logical(col, shift)
        return jnp.where(same & other & (row > col), d, zero)

    inv = jnp.where(eye, jnp.broadcast_to(recip_row, (n, n)), -(below(0) * recip_row) * recip_col)
    shift = 1
    while (1 << shift) < n:
        inv = inv - dot(inv, dot(below(shift), inv))
        shift += 1
    return inv


def split(x):
    hi = x.astype(BF16)
    return hi, (x - hi.astype(F32)).astype(BF16)


def bdot(a, b):
    return jnp.dot(a, b, preferred_element_type=F32)


def kernel(
    rows,
    cols,
    s_hbm,
    panel_hbm,
    given_hbm,
    diag_hbm,
    x_v,
    g_out,
    s_v,
    s_hi,
    s_lo,
    p_v,
    b_v,
    d_v,
    pt_v,
    inv_v,
    inv_b,
    lc,
    flip_v,
    flip_in,
    route_src,
    route_in,
    half_v,
    give_v,
    pair_in,
    agg_far,
    agg_near,
    agg_out,
    fin_in,
    prod_v,
    prod_in,
    quad_v,
    quad_in,
    cross_v,
    cross_in,
    ppair_v,
    ppair_in,
    pfull_v,
    loc,
    sc_s,
    sc_r,
    ag_s,
    ag_r,
    fl_s,
    fl_r,
    rt_s,
    rt_r,
    pr_s,
    pr_r,
    rs_s,
    rs_r,
    x_s,
    x_d,
    x_r,
    xp_s,
    xp_r,
    g_s,
    g_r,
):
    R, C = rows, cols
    Z = C // 2
    W = Z // 4
    SL = 8 * BLK // C
    NS = BLK // SL
    HALF = 4 * NS
    HR = 4 * BLK
    side = math.isqrt(R)
    r = lax.axis_index("row")
    c = lax.axis_index("col")
    z = c // 2
    k = c % 2

    def dev(row, chip, core):
        return (row, chip * 2 + core)

    hops = lambda d: min(d, side - d)
    steps = [(dx, dy) for dx in range(side) for dy in range(side) if dx + dy > 0]
    steps.sort(key=lambda d: -(hops(d[0]) + hops(d[1])))

    def at(step):
        dx, dy = step
        return ((r // side + dx) & (side - 1)) * side + ((r + dy) & (side - 1))

    sign = 1 - 2 * k

    def away(delta):
        return (z + sign * delta) & (Z - 1)

    def chip(delta):
        return dev(r, away(delta), k)

    def copy(src, dst, send, recv, device):
        return pltpu.make_async_remote_copy(
            src_ref=src,
            dst_ref=dst,
            send_sem=send,
            recv_sem=recv,
            device_id=device,
            device_id_type=MESH,
        )

    def wait(ref, sem):
        pltpu.make_async_copy(ref, ref, sem).wait()

    def offset_of(row, at):
        return (at - row // 2 + R // 4) & (Z - 1)

    def slice_in_half(o):
        m = o & (R // 2 - 1)
        return (2 * (m // NS) + o // (R // 2)) * NS + (m & (NS - 1))

    def slice_for(delta):
        return slice_in_half(offset_of(r, away(delta)))

    barrier = pltpu.get_barrier_semaphore()
    other = dev(r, z, 1 - k)
    for step in steps:
        pl.semaphore_signal(barrier, inc=1, device_id=(at(step), c), device_id_type=MESH)
    for i in range(W, 0, -1):
        for delta in (i, -i):
            for core in (0, 1):
                near_by = dev(r, (z + delta) & (Z - 1), core)
                pl.semaphore_signal(barrier, inc=1, device_id=near_by, device_id_type=MESH)
    pl.semaphore_signal(barrier, inc=1, device_id=other, device_id_type=MESH)

    cp_s = [pltpu.make_async_copy(s_hbm.at[a], s_v.at[a], loc.at[1 + a]) for a in range(8)]
    cp_panel = pltpu.make_async_copy(panel_hbm, p_v, loc.at[0])
    for one in cp_s:
        one.start()
    cp_panel.start()
    my_slice = slice_for(0)
    sid = k * HALF + my_slice
    cp_b = pltpu.make_async_copy(given_hbm.at[sid], b_v, loc.at[9])
    cp_b.start()
    cp_d = pltpu.make_async_copy(diag_hbm, d_v, loc.at[10])
    cp_d.start()

    greeted = R - 1 + 4 * W + 1
    owner = c & (R - 1)
    which = c // R
    own = owner == r

    def piece(s):
        return panel_hbm.at[(2 * (s // NS) + which) * NS + (s & (NS - 1))]

    @pl.when(own)
    def _():
        pl.semaphore_wait(barrier, greeted)
        for step in steps:
            s = at(step)
            copy(piece(s), lc.at[s], sc_s, sc_r, (s, c)).start()
        mine = pltpu.make_async_copy(piece(r), lc.at[r], loc.at[11])
        mine.start()
        mine.wait()

    for a in range(8):
        cp_s[a].wait()

        for b in range(4):
            hi, lo = split(s_v[a, pl.ds(b, BLK, stride=4), :])
            s_hi[pl.ds(a * BLK, BLK), pl.ds(b * BLK, BLK)] = hi
            s_lo[pl.ds(a * BLK, BLK), pl.ds(b * BLK, BLK)] = lo
    cp_panel.wait()
    for a in range(8):
        hi, lo = split(p_v[pl.ds(a * NS, NS)].reshape(BLK, BLK).T)
        pt_v[pl.ds(0, BLK), pl.ds(a * BLK, BLK)] = hi
        pt_v[pl.ds(BLK, BLK), pl.ds(a * BLK, BLK)] = lo
    for b in range(2):
        wide = pl.ds(b * 2 * BLK, 2 * BLK)
        both = bdot(pt_v[...], s_hi[:, wide])
        part = both[:BLK] + (both[BLK:] + bdot(pt_v[pl.ds(0, BLK), :], s_lo[:, wide]))
        flip_v[pl.ds(b * 2 * NS, 2 * NS)] = part.T.reshape(2 * NS, SL, BLK)

    @pl.when(jnp.logical_not(own))
    def _():
        pl.semaphore_wait(barrier, greeted)

    for step in steps:
        copy(flip_v.at[at(step)], flip_in.at[r], fl_s, fl_r, (at(step), c)).start()

    @pl.when(jnp.logical_not(own))
    def _():
        wait(lc.at[r], sc_r)

    for step in steps:
        copy(lc.at[r], lc.at[r], ag_s, ag_r, (at(step), c)).start()

    cp_d.wait()
    inv_v[...] = invert_lower(d_v[...])
    inv_hi, inv_lo = split(inv_v[...])
    inv_b[:, pl.ds(0, BLK)] = inv_hi
    inv_b[:, pl.ds(BLK, BLK)] = inv_lo

    wait(flip_in.at[pl.ds(0, R - 1)], fl_r)
    flip_in[r] = flip_v[r]
    total_flip = flip_in[0]
    for i in range(1, R):
        total_flip = total_flip + flip_in[i]
    route_src[...] = total_flip

    cross_part = dot_t(total_flip, lc[r])
    cp_b.wait()
    prod = dot_t(b_v[...], p_v[sid]) - (cross_part + cross_part.T)
    prod_v[...] = prod.reshape(R, BLK // R, BLK)
    for step in steps:
        copy(prod_v.at[at(step)], prod_in.at[r], g_s.at[0], g_r.at[0], (at(step), c)).start()

    wait(lc.at[pl.ds(0, R - 1)], ag_r)

    to_r = owner
    to_z = (z - R // 4 + (r & (R // 2 - 1))) & (Z - 1)
    to_k = r // (R // 2)
    to_self = (to_r == r) & (to_z == z) & (to_k == k)

    @pl.when(jnp.logical_not(to_self))
    def _():
        copy(route_src, route_in, rt_s, rt_r, dev(to_r, to_z, to_k)).start()

    @pl.when(to_self)
    def _():
        route_in[...] = route_src[...]

    w_hi, w_lo = split(lc[...].reshape(HR, BLK))
    w_both = jnp.concatenate([w_hi, w_lo], axis=1)

    def direct_half(base):
        at = pl.ds(pl.multiple_of(base * HR, HR), HR)
        both = bdot(s_hi[at, :], w_both)
        out = both[:, :BLK] + (both[:, BLK:] + bdot(s_lo[at, :], w_hi))
        return out.reshape(HALF, SL, BLK)

    give_v[...] = direct_half(1 - k)
    pair = copy(give_v, pair_in, pr_s, pr_r, other)
    pair.start()
    kept = direct_half(k)
    pair.wait()
    half_v[...] = kept + pair_in[...]

    for d in range(2 * W, W, -1):
        copy(half_v.at[slice_for(d)], agg_far.at[d - W - 1], rs_s, rs_r.at[0], chip(d - W)).start()
        if d < 2 * W:
            copy(
                half_v.at[slice_for(-d)], agg_near.at[d - W - 1], rs_s, rs_r.at[1], chip(W - d)
            ).start()

    pl.delay(RS_PAUSE)
    for d in range(W - 1, 0, -1):
        copy(half_v.at[slice_for(d)], fin_in.at[d - 1], rs_s, rs_r.at[2], chip(d)).start()
        copy(half_v.at[slice_for(-d)], fin_in.at[W + d - 2], rs_s, rs_r.at[2], chip(-d)).start()

    wait(prod_in.at[pl.ds(0, R - 1)], g_r.at[0])
    prod_in[r] = prod_v[r]
    acc = prod_in[0]
    for i in range(1, R):
        acc = acc + prod_in[i]
    group, lane = z // W, z & (W - 1)
    quad_v[...] = acc
    for i in range(1, W):
        mate = dev(r, group * W + ((lane + i) & (W - 1)), k)
        copy(quad_v, quad_in.at[lane], g_s.at[1], g_r.at[1], mate).start()

    wait(agg_far, rs_r.at[0])
    far = half_v[slice_for(W)]
    for i in range(W):
        far = far + agg_far[i]
    agg_out[0] = far
    copy(agg_out.at[0], fin_in.at[2 * W - 2], rs_s, rs_r.at[2], chip(W)).start()
    near = half_v[slice_for(-W)]
    if W > 1:
        wait(agg_near.at[pl.ds(0, W - 1)], rs_r.at[1])
        for i in range(W - 1):
            near = near + agg_near[i]
    agg_out[1] = near
    copy(agg_out.at[1], fin_in.at[2 * W - 1], rs_s, rs_r.at[2], chip(-W)).start()

    if W > 1:
        wait(quad_in.at[pl.ds(0, W - 1)], g_r.at[1])
    quad_in[lane] = quad_v[...]
    acc = quad_in[0]
    for i in range(1, W):
        acc = acc + quad_in[i]
    cross_v[...] = acc
    for i in range(1, 4):
        copy(cross_v, cross_in.at[group], g_s.at[2], g_r.at[2], chip(i * W)).start()

    @pl.when(jnp.logical_not(to_self))
    def _():
        wait(route_in, rt_r)

    wait(fin_in, rs_r.at[2])
    total = half_v[my_slice]
    for i in range(2 * W):
        total = total + fin_in[i]
    total = b_v[...] - (total + route_in[...])
    t_hi, t_lo = split(total)
    both = bdot(t_hi, inv_b[...])
    x_v[sid] = both[:, :BLK] + (both[:, BLK:] + bdot(t_lo, inv_b[:, pl.ds(0, BLK)]))

    def sid_at(delta):
        return k * HALF + slice_for(delta)

    def send_x(s, sem, device):
        copy(x_v.at[s], x_v.at[s], x_s, x_r.at[sem], device).start()

    def forward(s):
        copy(x_v.at[s], x_v.at[s], xp_s, xp_r, other).start()

    chosen = []

    def send_if(cond, s, sem, device):
        one = copy(x_v.at[s], x_v.at[s], x_d.at[len(chosen)], x_r.at[sem], device)
        chosen.append((cond, one))

        @pl.when(cond)
        def _():
            one.start()

    send_x(sid, W, chip(W))
    send_x(sid, 3 * W, chip(-W))
    for d in range(2 * W, W, -1):
        send_if(away(d) < FIRST, sid, d, chip(d))
        if d < 2 * W:
            send_if(away(-d) < FIRST, sid, 2 * W + d, chip(-d))
    forward(sid)
    pl.delay(AG_PAUSE)
    for d in range(W - 1, 0, -1):
        send_x(sid, d, chip(d))
        send_x(sid, 2 * W + d, chip(-d))

    wait(cross_in.at[pl.ds(0, 3)], g_r.at[2])
    cross_in[group] = cross_v[...]
    ppair_v[...] = (cross_in[0] + cross_in[1]) + (cross_in[2] + cross_in[3])
    hand = copy(ppair_v, ppair_in, g_s.at[3], g_r.at[3], other)
    hand.start()

    far_sid = sid_at(-W)
    wait(x_v.at[far_sid], x_r.at[W])
    for d in range(W, 0, -1):
        send_if(away(d) >= FIRST, far_sid, W + d, chip(d))
    near_sid = sid_at(W)
    wait(x_v.at[near_sid], x_r.at[3 * W])
    for d in range(W - 1, 0, -1):
        send_if(away(-d) >= FIRST, near_sid, 3 * W + d, chip(-d))
    hand.wait()
    pfull_v[r] = ppair_v[...] + ppair_in[...]
    for step in steps:
        copy(pfull_v.at[r], pfull_v.at[r], g_s.at[4], g_r.at[4], (at(step), c)).start()

    forward(far_sid)
    forward(near_sid)
    for d in range(1, W):
        wait(x_v.at[sid_at(-d)], x_r.at[d])
        forward(sid_at(-d))
        wait(x_v.at[sid_at(d)], x_r.at[2 * W + d])
        forward(sid_at(d))

    for d in range(1, W):
        wait(x_v.at[sid_at(-W - d)], x_r.at[W + d])
        forward(sid_at(-W - d))
        wait(x_v.at[sid_at(W + d)], x_r.at[3 * W + d])
        forward(sid_at(W + d))
    wait(x_v.at[sid_at(-2 * W)], x_r.at[2 * W])
    forward(sid_at(-2 * W))

    wait(pfull_v.at[pl.ds(0, R - 1)], g_r.at[4])
    gram = -dot_t(inv_v[...], pfull_v[...].reshape(BLK, BLK))
    row = lax.broadcasted_iota(jnp.int32, (BLK, BLK), 0)
    col = lax.broadcasted_iota(jnp.int32, (BLK, BLK), 1)
    g_out[...] = jnp.where(row >= col, gram, jnp.zeros_like(gram))

    @pl.when(own)
    def _():
        wait(lc.at[pl.ds(0, R - 1)], sc_s)

    wait(lc.at[pl.ds(0, R - 1)], ag_s)
    wait(flip_in.at[pl.ds(0, R - 1)], fl_s)

    @pl.when(jnp.logical_not(to_self))
    def _():
        wait(route_src, rt_s)

    wait(half_v.at[pl.ds(0, Z - 1)], rs_s)
    wait(half_v.at[pl.ds(0, 2 * W)], x_s)
    for cond, one in chosen:
        pl.when(cond)(one.wait_send)
    wait(prod_in.at[pl.ds(0, R - 1)], g_s.at[0])
    if W > 1:
        wait(quad_in.at[pl.ds(0, W - 1)], g_s.at[1])
    wait(cross_in.at[pl.ds(0, 3)], g_s.at[2])
    wait(pfull_v.at[pl.ds(0, R - 1)], g_s.at[4])
    wait(half_v, xp_s)
    wait(half_v, xp_r)


def write_out(x_v, g_v, x_hbm, g_hbm, sem):
    g_copy = pltpu.make_async_copy(g_v, g_hbm, sem.at[0])
    g_copy.start()
    x_copy = pltpu.make_async_copy(x_v, x_hbm, sem.at[1])
    x_copy.start()
    g_copy.wait()
    x_copy.wait()


def solution(mesh):
    R, C = mesh.shape["row"], mesh.shape["col"]
    Z = C // 2
    W = Z // 4
    SL = 8 * BLK // C
    NS = BLK // SL
    HALF = 4 * NS
    GL = BLK // R

    def per_device(trail_adjoint, panel, panel_adjoint, diag_block):
        any_spec = pl.BlockSpec(memory_space=pl.ANY)
        hbm = pl.BlockSpec(memory_space=pltpu.MemorySpace.HBM)
        vmem = pl.BlockSpec(memory_space=pltpu.MemorySpace.VMEM)
        vm = lambda *shape: pltpu.VMEM(shape, F32)
        dma = pltpu.SemaphoreType.DMA
        in_hbm = lambda x: pltpu.with_memory_space_constraint(x, pltpu.MemorySpace.HBM)
        x, gram = pl.pallas_call(
            functools.partial(kernel, R, C),
            out_shape=(
                jax.ShapeDtypeStruct((2 * HALF, SL, BLK), F32),
                jax.ShapeDtypeStruct((BLK, BLK), F32),
            ),
            in_specs=[hbm] * 4,
            out_specs=(vmem, vmem),
            scratch_shapes=[
                vm(8, 4 * BLK, BLK),
                pltpu.VMEM((8 * BLK, 4 * BLK), BF16),
                pltpu.VMEM((8 * BLK, 4 * BLK), BF16),
                vm(2 * HALF, SL, BLK),
                vm(SL, BLK),
                vm(BLK, BLK),
                pltpu.VMEM((2 * BLK, 8 * BLK), BF16),
                vm(BLK, BLK),
                pltpu.VMEM((BLK, 2 * BLK), BF16),
                vm(R, SL, BLK),
                vm(R, SL, BLK),
                vm(R, SL, BLK),
                vm(SL, BLK),
                vm(SL, BLK),
                vm(HALF, SL, BLK),
                vm(HALF, SL, BLK),
                vm(HALF, SL, BLK),
                vm(W, SL, BLK),
                vm(max(W - 1, 1), SL, BLK),
                vm(2, SL, BLK),
                vm(2 * W, SL, BLK),
                vm(R, GL, BLK),
                vm(R, GL, BLK),
                vm(GL, BLK),
                vm(W, GL, BLK),
                vm(GL, BLK),
                vm(4, GL, BLK),
                vm(GL, BLK),
                vm(GL, BLK),
                vm(R, GL, BLK),
                dma((12,)),
                dma(()),
                dma(()),
                dma(()),
                dma(()),
                dma(()),
                dma(()),
                dma(()),
                dma(()),
                dma(()),
                dma(()),
                dma(()),
                dma((3,)),
                dma(()),
                dma((4 * W - 2,)),
                dma((4 * W,)),
                dma(()),
                dma(()),
                dma((5,)),
                dma((5,)),
            ],
            compiler_params=pltpu.CompilerParams(
                collective_id=0, has_side_effects=True, vmem_limit_bytes=32 * 1024 * 1024
            ),
        )(
            in_hbm(trail_adjoint.reshape(8, 4 * BLK, BLK)),
            in_hbm(panel.reshape(2 * HALF, SL, BLK)),
            in_hbm(panel_adjoint.reshape(2 * HALF, SL, BLK)),
            in_hbm(diag_block),
        )
        x, gram = pl.pallas_call(
            write_out,
            out_shape=(
                jax.ShapeDtypeStruct((2 * HALF, SL, BLK), F32),
                jax.ShapeDtypeStruct((BLK, BLK), F32),
            ),
            in_specs=[any_spec] * 2,
            out_specs=(hbm, hbm),
            scratch_shapes=[dma((2,))],
            compiler_params=pltpu.CompilerParams(vmem_limit_bytes=8 * 1024 * 1024),
        )(x, gram)
        return x.reshape(8, BLK, BLK), gram

    return jax.shard_map(
        per_device,
        mesh=mesh,
        in_specs=(P(None, "row", None, "col"), P(None, "row", None), P(None, "row", None), P()),
        out_specs=(P(None, "row", None), P()),
        check_vma=False,
    )
```
